32 devices in a mesh: parts: 2 (over x), seq: 16 (over z, y, core).
Axes of the slice: x: 2, y: 2, z: 4, core: 2. Of those that a mesh axis runs over, the one named last changes fastest.
Arguments:
- prefix_latent: bfloat16 [61440, 512], P(('parts', 'seq')), parts along dimension 0, may hold values from -6 to 6
- block_order: int32 [480], P(('parts', 'seq')), parts along dimension 0, may hold values from 0 to 239, each once
- key_up: bfloat16 [512, 512], replicated, may hold values from -0.25 to 0.25
- value_up: bfloat16 [512, 512], replicated, may hold values from -0.25 to 0.25
- queries: bfloat16 [32, 4, 4096], P(('parts', 'seq')), parts along dimension 0, may hold values from -200 to 200
- new_keys: bfloat16 [32, 4, 512], P(('parts', 'seq')), parts along dimension 0, may hold values from -6 to 6
- new_values: bfloat16 [32, 4, 512], P(('parts', 'seq')), parts along dimension 0, may hold values from -6 to 6
- suffix_keys: bfloat16 [32, 4096, 512], P(('parts', 'seq')), parts along dimension 0, may hold values from -6 to 6
- suffix_values: bfloat16 [32, 4096, 512], P(('parts', 'seq')), parts along dimension 0, may hold values from -6 to 6
- suffix_len: int32 [32], P(('parts', 'seq')), parts along dimension 0, may hold values from 1 to 4096, 32768 in all
Outputs:
- attended: bfloat16 [32, 4, 4096], P(('parts', 'seq')), parts along dimension 0
The draws below stay inside these ranges and needn't reach their ends.
There are 2 independent parts, one for each index of `parts`. The reference program is written for one: setup_inputs(seed, part) draws one part's arguments, and reference() takes and returns one part's arrays. A program takes and returns all parts, laid end to end along the dimension named above; an argument that names none is the same for every part. Nothing has to cross between parts.
Inputs may be any that keep to these rules, and one draw needn't show every extreme that they name: A request's cache holds its first suffix_len entries; some request holds exactly 4096. `block_order`: each block position appears once.
All inputs are finite; a program needn't handle non-finite values. No bound on the sum of `suffix_len` on one device may be relied on, other than what follows from the above.
Results may differ from the reference program's by a relative error of at most 0.005.
The reference program's roundings to bfloat16 on the way count: a program that leaves them out, or rounds other values in their place, can miss the bound.
Values may be sent and summed in bfloat16 or wider, within the bound.
No kernel may reach another device: no remote copies, remote signals or barrier semaphores. Data moves between devices by JAX's collectives and lax.ppermute only.
A program may use at most 128 MiB of HBM per device.

```python
import math
import jax
import jax.numpy as jnp
import numpy as np
from jax import lax

HD = 128
QH = 32
KVH = 4
RANK = 512
BLK = 128
STEPS = 4
PRE_DEV = 1920
SUF = 4096
PREFIX = 30720
REQS = 16
NBLK = 240
N_SEQ = 16


def draw_queries(key, part):
    first = jax.random.fold_in(key, 0)
    shape = (REQS, STEPS, QH * HD)
    base = jnp.clip(jax.random.normal(first, shape, jnp.float32), -6.0, 6.0) * 2.5
    return base.astype(jnp.bfloat16)


def block_scale(rng, extent, shards, low, largest):
    loudness, own = 1.0, jax.random.fold_in(rng, 6)
    for axis_at, blocks in shards:
        draws = jnp.exp(jax.random.uniform(jax.random.fold_in(own, axis_at), (blocks,), jnp.float32, low / len(shards), largest / len(shards)))
        loudness = loudness * jnp.repeat(draws, extent[axis_at] // blocks).reshape([-1 if axis == axis_at else 1 for axis in range(len(extent))])
    return loudness


def split_up(number_of, total, bound, lean):
    weights = [(1 << 20) // math.isqrt(rank ** lean) + 1 for rank in range(2, number_of + 1)]
    surplus, counts = total - bound - (number_of - 1), [1] * (number_of - 1)
    while surplus > 0:
        candidates = [i for i in range(number_of - 1) if counts[i] < bound]
        pool, remaining = sum([weights[i] for i in candidates]), surplus
        for i in candidates:
            addition = min(bound - counts[i], max(1, remaining * weights[i] // pool), surplus)
            counts[i] = counts[i] + addition
            surplus = surplus - addition
    return np.array([bound] + counts)


def ragged(own_key, count, total, bound, lean):
    if count == 2:
        one = jax.random.randint(own_key, (), max(1, total - bound), min(bound, total - 1) + 1)
        return jnp.stack([one, total - one])
    sizes = jnp.asarray(split_up(count, total, bound, lean), jnp.int32)
    pairs = (count - 1) // 2
    donor, taker = sizes[1:1 + 2 * pairs:2], sizes[2:2 + 2 * pairs:2]
    margin = jnp.minimum(donor - 1, bound - taker)
    moved = jax.random.randint(jax.random.fold_in(own_key, 1), (pairs,), 0, 1 << 20) % (margin + 1)
    sizes = sizes.at[1:1 + 2 * pairs:2].set(donor - moved).at[2:2 + 2 * pairs:2].set(taker + moved)
    return sizes[jax.random.permutation(jax.random.fold_in(own_key, 2), count)]


def normal_values(key, shape, scale, most, pieces=(), kind=jnp.bfloat16):
    loudness = block_scale(key, shape, pieces, -0.22, 0.18) if pieces else 1.0
    array = jax.random.normal(key, shape, jnp.float32) * scale * loudness
    return jnp.minimum(jnp.maximum(array, -most), most).astype(kind)


def setup_inputs(seed: int = 0, part: int = 0) -> dict:
    arg_keys = jax.random.split(jax.random.key(seed), 11)
    part_keys = jax.random.split(jax.random.fold_in(arg_keys[10], part), 11)
    return {
        "prefix_latent": normal_values(part_keys[0], (PREFIX, RANK), 1.0, 6.0, ((0, 16),)),
        "block_order": jax.random.permutation(part_keys[1], NBLK).astype(jnp.int32),
        "key_up": normal_values(arg_keys[2], (RANK, KVH * HD), RANK ** -0.5, 0.25),
        "value_up": normal_values(arg_keys[3], (RANK, KVH * HD), RANK ** -0.5, 0.25),
        "queries": draw_queries(jax.random.fold_in(jax.random.fold_in(arg_keys[10], part), 71), part),
        "new_keys": normal_values(part_keys[5], (REQS, STEPS, KVH * HD), 1.0, 6.0, ((0, 16),)),
        "new_values": normal_values(part_keys[6], (REQS, STEPS, KVH * HD), 1.0, 6.0, ((0, 16),)),
        "suffix_keys": normal_values(part_keys[7], (REQS, SUF, KVH * HD), 1.0, 6.0, ((0, 16),)),
        "suffix_values": normal_values(part_keys[8], (REQS, SUF, KVH * HD), 1.0, 6.0, ((0, 16),)),
        "suffix_len": ragged(part_keys[9], REQS, REQS * SUF // 2, SUF, 0).astype(jnp.int32),
    }


def phase_table(half):
    index = np.arange(half)
    freq = 500000.0 ** (-2.0 * index / (2 * half))
    mult = np.floor(2.0 ** 24 * freq / (2 * np.pi)).astype(np.int64)
    return ((mult >> 12).astype(np.int32), (mult & 4095).astype(np.int32))

def rotate(values, position):
    half = values.shape[-1] // 2
    high, low = phase_table(half)
    spot = position[..., None]
    first = spot * jnp.asarray(low, dtype=jnp.int32)
    second = spot * jnp.asarray(high, dtype=jnp.int32) % 4096
    turns = (first + second * 4096) % 16777216
    angle = turns.astype(values.dtype) * (2.0 * math.pi / 16777216.0)
    cosine = jnp.cos(angle)[..., None, :]
    sine = jnp.sin(angle)[..., None, :]
    lower = values[..., :half]
    upper = values[..., half:]
    return jnp.concatenate([lower * cosine - upper * sine, upper * cosine + lower * sine], -1)

def rounded(values):
    return lax.optimization_barrier(values.astype(jnp.bfloat16)).astype(jnp.float32)

def reference(prefix_latent, block_order, key_up, value_up, queries, new_keys, new_values, suffix_keys, suffix_values, suffix_len):
    prefix = prefix_latent.shape[0]
    group = QH // KVH
    scale = 1.0 / math.sqrt(HD)
    rows = jnp.arange(prefix, dtype=jnp.int32)
    key_pos = block_order[rows // BLK] * BLK + rows % BLK
    keys = jnp.dot(prefix_latent, key_up, preferred_element_type=jnp.float32).reshape(prefix, KVH, HD)
    keys = rotate(keys, key_pos).astype(jnp.bfloat16)
    values = jnp.dot(prefix_latent, value_up, preferred_element_type=jnp.float32).astype(jnp.bfloat16)
    shard_keys = keys.astype(jnp.float32).reshape(N_SEQ, PRE_DEV, KVH, HD)
    shard_values = values.astype(jnp.float32).reshape(N_SEQ, PRE_DEV, KVH, HD)
    step_index = jnp.arange(STEPS, dtype=jnp.int32)
    query_pos = prefix + suffix_len[:, None] + step_index[None, :]
    query_rot = rotate(queries.astype(jnp.float32).reshape(REQS, STEPS, QH, HD), query_pos).astype(jnp.bfloat16)
    new_rot = rotate(new_keys.astype(jnp.float32).reshape(REQS, STEPS, KVH, HD), query_pos).astype(jnp.bfloat16)
    causal = (step_index[:, None] >= step_index[None, :])[:, None, None, :]
    slots = jnp.arange(SUF, dtype=jnp.int32)

    def one_request(item):
        query, fresh_key, fresh_value, cache_key, cache_value, length = item
        split = query.astype(jnp.float32).reshape(STEPS, KVH, group, HD)
        scores = jnp.einsum('tkgd,jpkd->tkgjp', split, shard_keys) * scale
        peak = lax.optimization_barrier(jnp.max(scores, -1))
        expo = jnp.exp(scores - peak[..., None])
        total = lax.optimization_barrier(jnp.sum(expo, -1))
        summed = jnp.einsum('tkgjp,jpkd->tkgjd', rounded(expo), shard_values)
        part = summed / total[..., None]
        top = lax.optimization_barrier(jnp.max(peak, 3))
        factor = total * jnp.exp(peak - top[..., None])
        numer = lax.optimization_barrier(jnp.sum(factor[..., None] * part, 3))
        denom = lax.optimization_barrier(jnp.sum(factor, 3))
        cache_k = cache_key.astype(jnp.float32).reshape(SUF, KVH, HD)
        cache_v = cache_value.astype(jnp.float32).reshape(SUF, KVH, HD)
        cache_scores = jnp.einsum('tkgd,pkd->tkgp', split, cache_k) * scale
        cache_scores = jnp.where(slots < length, cache_scores, -jnp.inf)
        fresh_k = fresh_key.astype(jnp.float32).reshape(STEPS, KVH, HD)
        fresh_v = fresh_value.astype(jnp.float32).reshape(STEPS, KVH, HD)
        fresh_scores = jnp.einsum('tkgd,ukd->tkgu', split, fresh_k) * scale
        fresh_scores = jnp.where(causal, fresh_scores, -jnp.inf)
        local_peak = jnp.maximum(lax.optimization_barrier(jnp.max(cache_scores, -1)), lax.optimization_barrier(jnp.max(fresh_scores, -1)))
        cache_exp = jnp.exp(cache_scores - local_peak[..., None])
        fresh_exp = jnp.exp(fresh_scores - local_peak[..., None])
        local_total = lax.optimization_barrier(jnp.sum(cache_exp, -1)) + lax.optimization_barrier(jnp.sum(fresh_exp, -1))
        local_numer = jnp.einsum('tkgp,pkd->tkgd', rounded(cache_exp), cache_v) + jnp.einsum('tkgu,ukd->tkgd', rounded(fresh_exp), fresh_v)
        biggest = jnp.maximum(top, local_peak)
        prefix_weight = jnp.exp(top - biggest)
        local_weight = jnp.exp(local_peak - biggest)
        result = (numer * prefix_weight[..., None] + local_numer * local_weight[..., None]) / (denom * prefix_weight + local_total * local_weight)[..., None]
        return result.reshape(STEPS, QH * HD).astype(jnp.bfloat16)
    return lax.map(one_request, (query_rot, new_rot, new_values, suffix_keys, suffix_values, suffix_len))
```

```python
import functools
import math

import jax
import jax.numpy as jnp
import numpy as np
from jax import lax
from jax.experimental import pallas as pl
from jax.experimental.pallas import tpu as pltpu
from jax.sharding import PartitionSpec as P

HD = 128
QH = 32
KVH = 4
BLK = 128
STEPS = 4
SUF = 4096
GROUP = QH // KVH
HALF_KV = KVH // 2
WIDE = HALF_KV * HD
KROWS = GROUP * STEPS
HROWS = HALF_KV * KROWS
ROWS = KVH * KROWS
PAY = HROWS + 16
SCALE = 1.0 / math.sqrt(HD)
EXP2 = SCALE * math.log2(math.e)
LOG2E = math.log2(math.e)
TURN = 2.0 * math.pi / 16777216.0
SUF_TILE = 1024
F32 = jnp.float32
BF16 = jnp.bfloat16


def multipliers():
    half = HD // 2
    index = np.arange(half)
    freq = 500000.0 ** (-2.0 * index / (2 * half))
    return np.floor(2.0**24 * freq / (2 * np.pi)).astype(np.int64)


def phase_rows():
    mult = np.tile(multipliers(), 2)
    table = np.zeros((8, HD), np.int32)
    table[0] = mult >> 12
    table[1] = mult & 4095
    return table


def row_tables():
    mult = np.tile(multipliers(), 2)
    turns = (np.arange(BLK)[:, None] * mult[None, :]) % 16777216
    angle = turns * (2.0 * np.pi / 16777216.0)
    sign = np.where(np.arange(HD) < HD // 2, -1.0, 1.0)
    return (np.cos(angle).astype(np.float32), (np.sin(angle) * sign).astype(np.float32))


def phases(spot, high, low):
    first = spot * low
    second = (spot * high) & 4095
    turns = (first + second * 4096) & 16777215
    return turns.astype(F32) * TURN


def lane_sign(shape):
    lane = lax.broadcasted_iota(jnp.int32, shape, len(shape) - 1)
    return jnp.where(lane < HD // 2, -1.0, 1.0).astype(F32)


def turn(x, cosine, sine):
    return x * cosine + pltpu.roll(x, HD // 2, axis=1) * sine


def query_kernel(prefix, count, len_ref, table_ref, q_ref, nk_ref, send_ref, own_ref, new_ref, rows_ref, nrows_ref):
    step = lax.broadcasted_iota(jnp.int32, (8, HD), 0) % STEPS
    spot = prefix + len_ref[0] + step
    angle = phases(spot, table_ref[0:1, :], table_ref[1:2, :])
    cosine = jnp.cos(angle)
    sine = jnp.sin(angle) * lane_sign((8, HD))
    q = q_ref[0].astype(F32)
    for h in range(QH):
        rows_ref[h * STEPS : (h + 1) * STEPS, :] = q[:, h * HD : (h + 1) * HD]
    for i in range(ROWS // 8):
        rows_ref[i * 8 : i * 8 + 8, :] = turn(rows_ref[i * 8 : i * 8 + 8, :], cosine, sine)
    rotated = rows_ref[...].astype(BF16)
    own_ref[...] = rotated
    for d in range(count):
        part = d % 2
        send_ref[d] = rotated[part * HROWS : (part + 1) * HROWS]
    nrows_ref[...] = jnp.zeros_like(nrows_ref)
    nk = nk_ref[0].astype(F32)
    for k in range(KVH):
        cut = slice(k * HD, (k + 1) * HD)
        nrows_ref[0:STEPS, cut] = turn(nk[:, cut], cosine[0:STEPS], sine[0:STEPS])
    new_ref[...] = nrows_ref[...].astype(BF16)


def rotate_queries(queries, new_keys, suffix_len, prefix, count):
    smem = pl.BlockSpec(memory_space=pltpu.SMEM)
    vmem = pl.BlockSpec(memory_space=pltpu.VMEM)
    return pl.pallas_call(
        functools.partial(query_kernel, prefix, count),
        out_shape=(
            jax.ShapeDtypeStruct((count, HROWS, HD), BF16),
            jax.ShapeDtypeStruct((ROWS, HD), BF16),
            jax.ShapeDtypeStruct((16, KVH * HD), BF16),
        ),
        in_specs=[smem, vmem, vmem, vmem],
        out_specs=(vmem, vmem, vmem),
        scratch_shapes=[pltpu.VMEM((ROWS, HD), F32), pltpu.VMEM((16, KVH * HD), F32)],
        name="rotate_queries",
    )(suffix_len, jnp.asarray(phase_rows()), queries, new_keys)


def project_kernel(
    blocks, core_ref, order_ref, lat_ref, ku_ref, vu_ref, table_ref, rc_ref, rs_ref, k_ref, v_ref, bc_ref, bs_ref
):
    step = pl.program_id(0)

    @pl.when(step == 0)
    def _():
        pad = bc_ref.shape[0]
        row = lax.broadcasted_iota(jnp.int32, (pad, HD), 0)
        spot = jnp.zeros((pad, HD), jnp.int32)
        for b in range(blocks):
            spot = jnp.where(row == b, order_ref[b], spot)
        angle = phases(spot * BLK, table_ref[0:1, :], table_ref[1:2, :])
        bc_ref[...] = jnp.cos(angle)
        bs_ref[...] = jnp.sin(angle) * lane_sign((pad, HD))

    lat = lat_ref[...]
    per = lat.shape[0] // BLK
    keys = jnp.dot(lat, ku_ref[...], preferred_element_type=F32)
    v_ref[...] = jnp.dot(lat, vu_ref[...], preferred_element_type=F32).astype(BF16)
    for i in range(per):
        b = step * per + i
        block_cos = bc_ref[pl.ds(b, 1), :]
        block_sin = bs_ref[pl.ds(b, 1), :]
        cosine = block_cos * rc_ref[...] - block_sin * rs_ref[...]
        sine = block_sin * rc_ref[...] + block_cos * rs_ref[...]
        for k in range(HALF_KV):
            cut = slice(k * HD, (k + 1) * HD)
            part = keys[i * BLK : (i + 1) * BLK, cut]
            k_ref[i * BLK : (i + 1) * BLK, cut] = turn(part, cosine, sine).astype(BF16)


def project(core, order, latent, key_up, value_up):
    pre_rows, rank = latent.shape
    blocks = pre_rows // BLK
    per = max(d for d in range(1, 6) if blocks % d == 0)
    tile = per * BLK
    rc, rs = row_tables()
    fixed = lambda i, c, o: (0, 0)
    half = lambda i, c, o: (0, c[0])
    tiles = lambda i, c, o: (i, 0)
    return pl.pallas_call(
        functools.partial(project_kernel, blocks),
        out_shape=(
            jax.ShapeDtypeStruct((pre_rows, WIDE), BF16),
            jax.ShapeDtypeStruct((pre_rows, WIDE), BF16),
        ),
        grid_spec=pltpu.PrefetchScalarGridSpec(
            num_scalar_prefetch=2,
            grid=(blocks // per,),
            in_specs=[
                pl.BlockSpec((tile, rank), tiles),
                pl.BlockSpec((rank, WIDE), half),
                pl.BlockSpec((rank, WIDE), half),
                pl.BlockSpec((8, HD), fixed),
                pl.BlockSpec((BLK, HD), fixed),
                pl.BlockSpec((BLK, HD), fixed),
            ],
            out_specs=[pl.BlockSpec((tile, WIDE), tiles), pl.BlockSpec((tile, WIDE), tiles)],
            scratch_shapes=[pltpu.VMEM((-(-blocks // 8) * 8, HD), F32)] * 2,
        ),
        cost_estimate=pl.CostEstimate(
            flops=4 * pre_rows * rank * WIDE, bytes_accessed=pre_rows * (rank + 2 * WIDE) * 2, transcendentals=0
        ),
        name="project",
    )(core, order, latent, key_up, value_up, jnp.asarray(phase_rows()), jnp.asarray(rc), jnp.asarray(rs))


def three(x):
    first = x.astype(BF16).astype(F32)
    rest = x - first
    second = rest.astype(BF16).astype(F32)
    return first, second, rest - second


def attend_kernel(q_ref, k0_ref, v0_ref, k1_ref, v1_ref, out_ref):
    reqs = q_ref.shape[0]
    nt = (((1,), (1,)), ((), ()))
    peaks, totals = [], []
    for k in range(HALF_KV):
        cut = slice(k * HD, (k + 1) * HD)
        q = q_ref[:, k * KROWS : (k + 1) * KROWS, :].reshape(reqs * KROWS, HD)
        s0 = lax.dot_general(q, k0_ref[:, cut], nt, preferred_element_type=F32)
        s1 = lax.dot_general(q, k1_ref[:, cut], nt, preferred_element_type=F32)
        peak = jnp.maximum(jnp.max(s0, -1, keepdims=True), jnp.max(s1, -1, keepdims=True))
        e0 = jnp.exp2((s0 - peak) * EXP2)
        e1 = jnp.exp2((s1 - peak) * EXP2)
        total = jnp.sum(e0, -1, keepdims=True) + jnp.sum(e1, -1, keepdims=True)
        o = jnp.dot(e0.astype(BF16), v0_ref[:, cut], preferred_element_type=F32)
        o = o + jnp.dot(e1.astype(BF16), v1_ref[:, cut], preferred_element_type=F32)
        o = o / total
        out_ref[:, k * KROWS : (k + 1) * KROWS, :] = o.astype(BF16).reshape(reqs, KROWS, HD)
        peaks.append(peak * SCALE)
        totals.append(total)
    row = lax.broadcasted_iota(jnp.int32, (KROWS, HD), 0)
    lane = lax.broadcasted_iota(jnp.int32, (KROWS, HD), 1)
    place = lax.broadcasted_iota(jnp.int32, (16, HD), 0)
    for r in range(reqs):
        cut = slice(r * KROWS, (r + 1) * KROWS)
        lines = []
        for parts in (peaks, totals):
            line = jnp.zeros((1, HD), F32)
            for k in range(HALF_KV):
                spread = jnp.where(lane == row + k * KROWS, parts[k][cut], 0.0)
                line = line + jnp.sum(spread, 0, keepdims=True)
            lines.extend(three(line))
        stats = jnp.zeros((16, HD), F32)
        for i, line in enumerate(lines):
            stats = jnp.where(place == i, line, stats)
        out_ref[r, HROWS:PAY, :] = stats.astype(BF16)


def attend(q, k0, v0, k1, v1):
    count = q.shape[0]
    pre_rows = k0.shape[0]
    per = math.gcd(count, 4)
    fixed = lambda i: (0, 0)
    kv = pl.BlockSpec((pre_rows, WIDE), fixed)
    return pl.pallas_call(
        attend_kernel,
        out_shape=jax.ShapeDtypeStruct((count, PAY, HD), BF16),
        grid=(count // per,),
        in_specs=[pl.BlockSpec((per, HROWS, HD), lambda i: (i, 0, 0)), kv, kv, kv, kv],
        out_specs=pl.BlockSpec((per, PAY, HD), lambda i: (i, 0, 0)),
        compiler_params=pltpu.CompilerParams(vmem_limit_bytes=40 << 20),
        cost_estimate=pl.CostEstimate(
            flops=8 * count * HROWS * HD * pre_rows,
            bytes_accessed=8 * pre_rows * WIDE,
            transcendentals=2 * count * HROWS * pre_rows,
        ),
        name="attend",
    )(q, k0, v0, k1, v1)


def suffix_kernel(len_ref, q_ref, nk_ref, nv_ref, k_ref, v_ref, acc_ref, peak_ref, total_ref):
    step = pl.program_id(0)
    length = len_ref[0]
    tile = k_ref.shape[1]
    nt = (((1,), (1,)), ((), ()))

    def scores(keys):
        return jnp.concatenate(
            [
                lax.dot_general(
                    q_ref[k * KROWS : (k + 1) * KROWS, :],
                    keys[:, k * HD : (k + 1) * HD],
                    nt,
                    preferred_element_type=F32,
                )
                for k in range(KVH)
            ],
            0,
        )

    def weigh(probs, values):
        probs = probs.astype(BF16)
        return jnp.concatenate(
            [
                jnp.dot(
                    probs[k * KROWS : (k + 1) * KROWS],
                    values[:, k * HD : (k + 1) * HD],
                    preferred_element_type=F32,
                )
                for k in range(KVH)
            ],
            0,
        )

    @pl.when(step == 0)
    def _():
        s = scores(nk_ref[...])
        row = lax.broadcasted_iota(jnp.int32, s.shape, 0) % STEPS
        lane = lax.broadcasted_iota(jnp.int32, s.shape, 1)
        s = jnp.where(lane <= row, s, -jnp.inf)
        peak = jnp.max(s, -1, keepdims=True)
        e = jnp.exp2((s - peak) * EXP2)
        acc_ref[...] = weigh(e, nv_ref[...])
        peak_ref[...] = jnp.broadcast_to(peak, peak_ref.shape)
        total_ref[...] = jnp.broadcast_to(jnp.sum(e, -1, keepdims=True), total_ref.shape)

    @pl.when(step * tile < length)
    def _():
        s = scores(k_ref[0])
        spot = step * tile + lax.broadcasted_iota(jnp.int32, s.shape, 1)
        s = jnp.where(spot < length, s, -jnp.inf)
        old = peak_ref[:, 0:1]
        peak = jnp.maximum(old, jnp.max(s, -1, keepdims=True))
        keep = jnp.exp2((old - peak) * EXP2)
        e = jnp.exp2((s - peak) * EXP2)
        acc_ref[...] = acc_ref[...] * keep + weigh(e, v_ref[0])
        total_ref[...] = total_ref[...] * keep + jnp.sum(e, -1, keepdims=True)
        peak_ref[...] = jnp.broadcast_to(peak, peak_ref.shape)

    @pl.when(step == pl.num_programs(0) - 1)
    def _():
        peak_ref[...] = peak_ref[...] * SCALE


def suffix(length, q, new_rot, new_values, keys, values):
    tile = SUF_TILE
    fixed = lambda i, n: (0, 0)
    walk = lambda i, n: (0, jnp.minimum(i, (n[0] - 1) // tile), 0)
    out = jax.ShapeDtypeStruct((ROWS, HD), F32)
    return pl.pallas_call(
        suffix_kernel,
        out_shape=(out, out, out),
        grid_spec=pltpu.PrefetchScalarGridSpec(
            num_scalar_prefetch=1,
            grid=(SUF // tile,),
            in_specs=[
                pl.BlockSpec((ROWS, HD), fixed),
                pl.BlockSpec((16, KVH * HD), fixed),
                pl.BlockSpec((16, KVH * HD), fixed),
                pl.BlockSpec((1, tile, KVH * HD), walk),
                pl.BlockSpec((1, tile, KVH * HD), walk),
            ],
            out_specs=[pl.BlockSpec((ROWS, HD), fixed)] * 3,
        ),
        cost_estimate=pl.CostEstimate(
            flops=4 * ROWS * SUF * HD, bytes_accessed=4 * SUF * KVH * HD, transcendentals=ROWS * SUF
        ),
        name="suffix",
    )(length, q, new_rot, new_values, keys, values)


def combine_kernel(got_ref, acc_ref, peak_ref, total_ref, out_ref):
    count = got_ref.shape[0]
    row = lax.broadcasted_iota(jnp.int32, (HROWS, HD), 0)
    lane = lax.broadcasted_iota(jnp.int32, (HROWS, HD), 1)
    eye = row == lane

    def column(line):
        return jnp.sum(jnp.where(eye, line, 0.0), -1, keepdims=True)

    for part in range(2):
        sources = range(part, count, 2)
        stats = [got_ref[j, HROWS:PAY, :].astype(F32) for j in sources]
        peaks = [s[0:1] + s[1:2] + s[2:3] for s in stats]
        totals = [s[3:4] + s[4:5] + s[5:6] for s in stats]
        top = functools.reduce(jnp.maximum, peaks)
        factors = [t * jnp.exp2((p - top) * LOG2E) for p, t in zip(peaks, totals)]
        denom = column(sum(factors))
        top = column(top)
        numer = jnp.zeros((HROWS, HD), F32)
        for j, factor in zip(sources, factors):
            numer = numer + column(factor) * got_ref[j, 0:HROWS, :].astype(F32)
        cut = slice(part * HROWS, (part + 1) * HROWS)
        near = peak_ref[cut, :]
        big = jnp.maximum(top, near)
        far_weight = jnp.exp2((top - big) * LOG2E)
        near_weight = jnp.exp2((near - big) * LOG2E)
        result = (numer * far_weight + acc_ref[cut, :] * near_weight) / (
            denom * far_weight + total_ref[cut, :] * near_weight
        )
        for h in range(HROWS // STEPS):
            at = part * (HROWS // STEPS) + h
            out_ref[0, :, at * HD : (at + 1) * HD] = result[h * STEPS : (h + 1) * STEPS].astype(BF16)


def combine(got, acc, peak, total):
    vmem = pl.BlockSpec(memory_space=pltpu.VMEM)
    return pl.pallas_call(
        combine_kernel,
        out_shape=jax.ShapeDtypeStruct((1, STEPS, QH * HD), BF16),
        in_specs=[vmem] * 4,
        out_specs=vmem,
        name="combine",
    )(got, acc, peak, total)


def local(
    prefix_latent,
    block_order,
    key_up,
    value_up,
    queries,
    new_keys,
    new_values,
    suffix_keys,
    suffix_values,
    suffix_len,
):
    count = lax.axis_size("seq")
    prefix = prefix_latent.shape[0] * count
    core = (lax.axis_index("seq") % 2).astype(jnp.int32)[None]
    swap = [(i, i ^ 1) for i in range(count)]
    send, own, new_rot = rotate_queries(queries, new_keys, suffix_len, prefix, count)
    other_latent = lax.ppermute(prefix_latent, "seq", swap)
    other_order = lax.ppermute(block_order, "seq", swap)
    gathered = lax.all_to_all(send, "seq", split_axis=0, concat_axis=0, tiled=True)
    k0, v0 = project(core, block_order, prefix_latent, key_up, value_up)
    k1, v1 = project(core, other_order, other_latent, key_up, value_up)
    parts = attend(gathered, k0, v0, k1, v1)
    got = lax.all_to_all(parts, "seq", split_axis=0, concat_axis=0, tiled=True)
    new_pad = jnp.pad(new_values[0], ((0, 16 - STEPS), (0, 0)))
    acc, peak, total = suffix(suffix_len, own, new_rot, new_pad, suffix_keys, suffix_values)
    return combine(got, acc, peak, total)


def solution(mesh):
    placed = (
        P(("parts", "seq"), None),
        P(("parts", "seq")),
        P(),
        P(),
        P(("parts", "seq"), None, None),
        P(("parts", "seq"), None, None),
        P(("parts", "seq"), None, None),
        P(("parts", "seq"), None, None),
        P(("parts", "seq"), None, None),
        P(("parts", "seq")),
    )
    return jax.shard_map(
        local,
        mesh=mesh,
        in_specs=placed,
        out_specs=P(("parts", "seq"), None, None),
        check_vma=False,
    )
```

```python
import functools
import math

import jax
import jax.numpy as jnp
import numpy as np
from jax import lax
from jax.experimental import pallas as pl
from jax.experimental.pallas import tpu as pltpu
from jax.sharding import PartitionSpec as P

HD = 128
QH = 32
KVH = 4
BLK = 128
STEPS = 4
SUF = 4096
GROUP = QH // KVH
HALF_KV = KVH // 2
WIDE = HALF_KV * HD
KROWS = GROUP * STEPS
HROWS = HALF_KV * KROWS
ROWS = KVH * KROWS
PAY = HROWS + 8
SCALE = 1.0 / math.sqrt(HD)
EXP2 = SCALE * math.log2(math.e)
LOG2E = math.log2(math.e)
TURN = 2.0 * math.pi / 16777216.0
SUF_TILE = 1024
PER = 5
Q_GROUP = 16
CHUNKS = 5
F32 = jnp.float32
BF16 = jnp.bfloat16


def multipliers():
    half = HD // 2
    index = np.arange(half)
    freq = 500000.0 ** (-2.0 * index / (2 * half))
    return np.floor(2.0**24 * freq / (2 * np.pi)).astype(np.int64)


def phase_rows():
    mult = np.tile(multipliers(), 2)
    table = np.zeros((8, HD), np.int32)
    table[0] = mult >> 12
    table[1] = mult & 4095
    return table


def row_tables():
    mult = np.tile(multipliers(), 2)
    turns = (np.arange(BLK)[:, None] * mult[None, :]) % 16777216
    angle = turns * (2.0 * np.pi / 16777216.0)
    sign = np.where(np.arange(HD) < HD // 2, -1.0, 1.0)
    return (np.cos(angle).astype(np.float32), (np.sin(angle) * sign).astype(np.float32))


def phases(spot, high, low):
    first = spot * low
    second = (spot * high) & 4095
    turns = (first + second * 4096) & 16777215
    return turns.astype(F32) * TURN


def lane_sign(shape):
    lane = lax.broadcasted_iota(jnp.int32, shape, len(shape) - 1)
    return jnp.where(lane < HD // 2, -1.0, 1.0).astype(F32)


def turn(x, cosine, sine):
    return x * cosine + pltpu.roll(x, HD // 2, axis=1) * sine


def query_kernel(prefix, count, len_ref, table_ref, q_ref, nk_ref, send_ref, own_ref, new_ref, rows_ref, nrows_ref):
    step = lax.broadcasted_iota(jnp.int32, (8, HD), 0) % STEPS
    spot = prefix + len_ref[0] + step
    angle = phases(spot, table_ref[0:1, :], table_ref[1:2, :])
    cosine = jnp.cos(angle)
    sine = jnp.sin(angle) * lane_sign((8, HD))
    q = q_ref[0].astype(F32)
    for h in range(QH):
        rows_ref[h * STEPS : (h + 1) * STEPS, :] = q[:, h * HD : (h + 1) * HD]
    for i in range(ROWS // 8):
        rows_ref[i * 8 : i * 8 + 8, :] = turn(rows_ref[i * 8 : i * 8 + 8, :], cosine, sine)
    rotated = rows_ref[...].astype(BF16)
    own_ref[...] = rotated
    for d in range(count):
        part = d % 2
        send_ref[d] = rotated[part * HROWS : (part + 1) * HROWS]
    nrows_ref[...] = jnp.zeros_like(nrows_ref)
    nk = nk_ref[0].astype(F32)
    for k in range(KVH):
        cut = slice(k * HD, (k + 1) * HD)
        nrows_ref[0:STEPS, cut] = turn(nk[:, cut], cosine[0:STEPS], sine[0:STEPS])
    new_ref[...] = nrows_ref[...].astype(BF16)


def rotate_queries(queries, new_keys, suffix_len, prefix, count):
    smem = pl.BlockSpec(memory_space=pltpu.SMEM)
    vmem = pl.BlockSpec(memory_space=pltpu.VMEM)
    return pl.pallas_call(
        functools.partial(query_kernel, prefix, count),
        out_shape=(
            jax.ShapeDtypeStruct((count, HROWS, HD), BF16),
            jax.ShapeDtypeStruct((ROWS, HD), BF16),
            jax.ShapeDtypeStruct((16, KVH * HD), BF16),
        ),
        in_specs=[smem, vmem, vmem, vmem],
        out_specs=(vmem, vmem, vmem),
        scratch_shapes=[pltpu.VMEM((ROWS, HD), F32), pltpu.VMEM((16, KVH * HD), F32)],
        name="rotate_queries",
    )(suffix_len, jnp.asarray(phase_rows()), queries, new_keys)


def project_kernel(
    core_ref,
    order0_ref,
    order1_ref,
    lat0_hbm,
    lat1_hbm,
    ku_hbm,
    vu_hbm,
    table_ref,
    rc_ref,
    rs_ref,
    k_hbm,
    v_hbm,
    bc_ref,
    bs_ref,
    lat_ref,
    ku_ref,
    vu_ref,
    k_ref,
    v_ref,
    in_sem,
    w_sem,
    out_sem,
):
    pre_rows = lat0_hbm.shape[0]
    blocks = pre_rows // BLK
    per = max(d for d in range(1, PER + 1) if blocks % d == 0)
    chunks = blocks // per
    size = per * BLK
    mine = pl.ds(pl.multiple_of(core_ref[0] * WIDE, WIDE), WIDE)
    loads = [
        pltpu.make_async_copy(ku_hbm.at[:, mine], ku_ref, w_sem.at[0]),
        pltpu.make_async_copy(vu_hbm.at[:, mine], vu_ref, w_sem.at[1]),
    ]
    fetches = []
    for side, source in enumerate((lat0_hbm, lat1_hbm)):
        for c in range(chunks):
            at = pl.ds(c * size, size)
            slot = side * chunks + c
            fetches.append(pltpu.make_async_copy(source.at[at], lat_ref.at[pl.ds(slot * size, size)], in_sem.at[slot]))
    loads[0].start()
    fetches[0].start()
    loads[1].start()
    for fetch in fetches[1:]:
        fetch.start()
    pad = bc_ref.shape[0]
    row = lax.broadcasted_iota(jnp.int32, (pad, HD), 0)
    spot = jnp.zeros((pad, HD), jnp.int32)
    for side, order_ref in enumerate((order0_ref, order1_ref)):
        for b in range(blocks):
            spot = jnp.where(row == side * blocks + b, order_ref[b], spot)
    angle = phases(spot * BLK, table_ref[0:1, :], table_ref[1:2, :])
    bc_ref[...] = jnp.cos(angle)
    bs_ref[...] = jnp.sin(angle) * lane_sign((pad, HD))
    loads[0].wait()
    loads[1].wait()
    stores = []
    for slot in range(2 * chunks):
        at = pl.ds(slot * size, size)
        fetches[slot].wait()
        lat = lat_ref[at, :]
        keys = jnp.dot(lat, ku_ref[...], preferred_element_type=F32)
        values = jnp.dot(lat, vu_ref[...], preferred_element_type=F32).astype(BF16)
        for k in range(HALF_KV):
            v_ref[k, at, :] = values[:, k * HD : (k + 1) * HD]
        for i in range(per):
            b = slot * per + i
            block_cos = bc_ref[b : b + 1, :]
            block_sin = bs_ref[b : b + 1, :]
            cosine = block_cos * rc_ref[...] - block_sin * rs_ref[...]
            sine = block_sin * rc_ref[...] + block_cos * rs_ref[...]
            for k in range(HALF_KV):
                part = keys[i * BLK : (i + 1) * BLK, k * HD : (k + 1) * HD]
                k_ref[k, b * BLK : (b + 1) * BLK, :] = turn(part, cosine, sine).astype(BF16)
        for k in range(HALF_KV):
            for kind, (source, target) in enumerate(((k_ref, k_hbm), (v_ref, v_hbm))):
                sem = out_sem.at[(slot * HALF_KV + k) * 2 + kind]
                store = pltpu.make_async_copy(source.at[k, at], target.at[k, at], sem)
                store.start()
                stores.append(store)
    for store in stores:
        store.wait()


def project(core, order0, order1, latent0, latent1, key_up, value_up):
    pre_rows, rank = latent0.shape
    blocks = pre_rows // BLK
    per = max(d for d in range(1, PER + 1) if blocks % d == 0)
    slots = 2 * blocks // per
    rows = 2 * pre_rows
    rc, rs = row_tables()
    smem = pl.BlockSpec(memory_space=pltpu.SMEM)
    vmem = pl.BlockSpec(memory_space=pltpu.VMEM)
    hbm = pl.BlockSpec(memory_space=pl.ANY)
    pad = -(-2 * blocks // 8) * 8
    out = jax.ShapeDtypeStruct((HALF_KV, rows, HD), BF16)
    return pl.pallas_call(
        project_kernel,
        out_shape=(out, out),
        in_specs=[smem, smem, smem, hbm, hbm, hbm, hbm, vmem, vmem, vmem],
        out_specs=(hbm, hbm),
        scratch_shapes=[
            pltpu.VMEM((pad, HD), F32),
            pltpu.VMEM((pad, HD), F32),
            pltpu.VMEM((rows, rank), BF16),
            pltpu.VMEM((rank, WIDE), BF16),
            pltpu.VMEM((rank, WIDE), BF16),
            pltpu.VMEM((HALF_KV, rows, HD), BF16),
            pltpu.VMEM((HALF_KV, rows, HD), BF16),
            pltpu.SemaphoreType.DMA((slots,)),
            pltpu.SemaphoreType.DMA((2,)),
            pltpu.SemaphoreType.DMA((slots * HALF_KV * 2,)),
        ],
        cost_estimate=pl.CostEstimate(
            flops=4 * rows * rank * WIDE, bytes_accessed=rows * (rank + 2 * WIDE) * 2, transcendentals=0
        ),
        compiler_params=pltpu.CompilerParams(vmem_limit_bytes=(64 << 20) - 2200000),
        name="project",
    )(core, order0, order1, far(latent0), latent1, far(key_up), far(value_up), jnp.asarray(phase_rows()), jnp.asarray(rc), jnp.asarray(rs))


def far(x):
    return pltpu.with_memory_space_constraint(x, pltpu.HBM)


def three(x):
    first = x.astype(BF16).astype(F32)
    rest = x - first
    second = rest.astype(BF16).astype(F32)
    return first, second, rest - second


def attend_kernel(per, q_ref, k_hbm, v_hbm, out_ref, k_ref, v_ref, stat_ref, sem):
    nt = (((1,), (1,)), ((), ()))
    row = lax.broadcasted_iota(jnp.int32, (KROWS, HD), 0)
    lane = lax.broadcasted_iota(jnp.int32, (KROWS, HD), 1)
    place = lax.broadcasted_iota(jnp.int32, (8, HD), 0)
    size = k_hbm.shape[1] // CHUNKS
    fetches = []
    for k in range(HALF_KV):
        for kind, (source, target) in enumerate(((k_hbm, k_ref), (v_hbm, v_ref))):
            for c in range(CHUNKS):
                at = pl.ds(c * size, size)
                slot = (k * 2 + kind) * CHUNKS + c
                fetches.append(pltpu.make_async_copy(source.at[k, at], target.at[k, at], sem.at[slot]))
    for fetch in fetches:
        fetch.start()

    for k in range(HALF_KV):
        for fetch in fetches[k * 2 * CHUNKS : (k + 1) * 2 * CHUNKS]:
            fetch.wait()

        def group(g, k=k):
            base = g * per
            rows = slice(k * KROWS, (k + 1) * KROWS)
            q = q_ref[pl.ds(base, per), rows, :].reshape(per * KROWS, HD)
            width = k_hbm.shape[1] // CHUNKS

            def score(c):
                return lax.dot_general(q, k_ref[k, c * width : (c + 1) * width, :], nt, preferred_element_type=F32)

            ahead = score(0)
            for c in range(CHUNKS):
                s = ahead
                if c + 1 < CHUNKS:
                    ahead = score(c + 1)
                best = jnp.max(s, -1, keepdims=True)
                if c:
                    best = jnp.maximum(peak, best)
                    keep = jnp.exp2((peak - best) * EXP2)
                e = jnp.exp2((s - best) * EXP2)
                here = jnp.sum(e, -1, keepdims=True)
                o = jnp.dot(e.astype(BF16), v_ref[k, c * width : (c + 1) * width, :], preferred_element_type=F32)
                total = total * keep + here if c else here
                acc = acc * keep + o if c else o
                peak = best
            o = acc / total
            out_ref[pl.ds(base, per), rows, :] = o.astype(BF16).reshape(per, KROWS, HD)
            peak = peak * SCALE
            for r in range(per):
                cut = slice(r * KROWS, (r + 1) * KROWS)
                stats = jnp.zeros((8, HD), F32)
                for i, part in enumerate((peak, total)):
                    spread = jnp.where(lane == row + k * KROWS, part[cut], 0.0)
                    for j, line in enumerate(three(jnp.sum(spread, 0, keepdims=True))):
                        stats = jnp.where(place == 3 * i + j, line, stats)
                if k == 0:
                    stat_ref[base + r] = stats
                else:
                    out_ref[base + r, HROWS:PAY, :] = (stat_ref[base + r] + stats).astype(BF16)

        pl.loop(0, q_ref.shape[0] // per)(group)


def attend(q, keys, values):
    count = q.shape[0]
    rows = keys.shape[1]
    vmem = pl.BlockSpec(memory_space=pltpu.VMEM)
    hbm = pl.BlockSpec(memory_space=pl.ANY)
    return pl.pallas_call(
        functools.partial(attend_kernel, math.gcd(count, Q_GROUP)),
        out_shape=jax.ShapeDtypeStruct((count, PAY, HD), BF16),
        in_specs=[vmem, hbm, hbm],
        out_specs=vmem,
        scratch_shapes=[
            pltpu.VMEM((HALF_KV, rows, HD), BF16),
            pltpu.VMEM((HALF_KV, rows, HD), BF16),
            pltpu.VMEM((count, 8, HD), F32),
            pltpu.SemaphoreType.DMA((4 * CHUNKS,)),
        ],
        compiler_params=pltpu.CompilerParams(vmem_limit_bytes=48 << 20),
        cost_estimate=pl.CostEstimate(
            flops=4 * count * HROWS * HD * rows,
            bytes_accessed=4 * rows * WIDE,
            transcendentals=count * HROWS * rows,
        ),
        name="attend",
    )(q, far(keys), far(values))


def suffix_kernel(len_ref, q_ref, nk_ref, nv_ref, k_ref, v_ref, acc_ref, peak_ref, total_ref):
    step = pl.program_id(0)
    length = len_ref[0]
    tile = k_ref.shape[1]
    nt = (((1,), (1,)), ((), ()))

    def scores(keys):
        return jnp.concatenate(
            [
                lax.dot_general(
                    q_ref[k * KROWS : (k + 1) * KROWS, :],
                    keys[:, k * HD : (k + 1) * HD],
                    nt,
                    preferred_element_type=F32,
                )
                for k in range(KVH)
            ],
            0,
        )

    def weigh(probs, values):
        probs = probs.astype(BF16)
        return jnp.concatenate(
            [
                jnp.dot(
                    probs[k * KROWS : (k + 1) * KROWS],
                    values[:, k * HD : (k + 1) * HD],
                    preferred_element_type=F32,
                )
                for k in range(KVH)
            ],
            0,
        )

    @pl.when(step == 0)
    def _():
        s = scores(nk_ref[...])
        row = lax.broadcasted_iota(jnp.int32, s.shape, 0) % STEPS
        lane = lax.broadcasted_iota(jnp.int32, s.shape, 1)
        s = jnp.where(lane <= row, s, -jnp.inf)
        peak = jnp.max(s, -1, keepdims=True)
        e = jnp.exp2((s - peak) * EXP2)
        acc_ref[...] = weigh(e, nv_ref[...])
        peak_ref[...] = jnp.broadcast_to(peak, peak_ref.shape)
        total_ref[...] = jnp.broadcast_to(jnp.sum(e, -1, keepdims=True), total_ref.shape)

    @pl.when(step * tile < length)
    def _():
        s = scores(k_ref[0])
        spot = step * tile + lax.broadcasted_iota(jnp.int32, s.shape, 1)
        s = jnp.where(spot < length, s, -jnp.inf)
        old = peak_ref[:, 0:1]
        peak = jnp.maximum(old, jnp.max(s, -1, keepdims=True))
        keep = jnp.exp2((old - peak) * EXP2)
        e = jnp.exp2((s - peak) * EXP2)
        acc_ref[...] = acc_ref[...] * keep + weigh(e, v_ref[0])
        total_ref[...] = total_ref[...] * keep + jnp.sum(e, -1, keepdims=True)
        peak_ref[...] = jnp.broadcast_to(peak, peak_ref.shape)

    @pl.when(step == pl.num_programs(0) - 1)
    def _():
        peak_ref[...] = peak_ref[...] * SCALE


def suffix(length, q, new_rot, new_values, keys, values):
    tile = SUF_TILE
    fixed = lambda i, n: (0, 0)
    walk = lambda i, n: (0, jnp.minimum(i, (n[0] - 1) // tile), 0)
    out = jax.ShapeDtypeStruct((ROWS, HD), F32)
    return pl.pallas_call(
        suffix_kernel,
        out_shape=(out, out, out),
        grid_spec=pltpu.PrefetchScalarGridSpec(
            num_scalar_prefetch=1,
            grid=(SUF // tile,),
            in_specs=[
                pl.BlockSpec((ROWS, HD), fixed),
                pl.BlockSpec((16, KVH * HD), fixed),
                pl.BlockSpec((16, KVH * HD), fixed),
                pl.BlockSpec((1, tile, KVH * HD), walk),
                pl.BlockSpec((1, tile, KVH * HD), walk),
            ],
            out_specs=[pl.BlockSpec((ROWS, HD), fixed)] * 3,
        ),
        cost_estimate=pl.CostEstimate(
            flops=4 * ROWS * SUF * HD, bytes_accessed=4 * SUF * KVH * HD, transcendentals=ROWS * SUF
        ),
        compiler_params=pltpu.CompilerParams(vmem_limit_bytes=40 << 20),
        name="suffix",
    )(length, q, new_rot, new_values, far(keys), far(values))


def combine_kernel(got_ref, acc_ref, peak_ref, total_ref, out_ref):
    count = got_ref.shape[0]
    row = lax.broadcasted_iota(jnp.int32, (HROWS, HD), 0)
    lane = lax.broadcasted_iota(jnp.int32, (HROWS, HD), 1)
    eye = row == lane

    def column(line):
        return jnp.sum(jnp.where(eye, line, 0.0), -1, keepdims=True)

    for part in range(2):
        sources = range(part, count, 2)
        stats = [got_ref[j, HROWS:PAY, :].astype(F32) for j in sources]
        peaks = [s[0:1] + s[1:2] + s[2:3] for s in stats]
        totals = [s[3:4] + s[4:5] + s[5:6] for s in stats]
        top = functools.reduce(jnp.maximum, peaks)
        factors = [t * jnp.exp2((p - top) * LOG2E) for p, t in zip(peaks, totals)]
        denom = column(sum(factors))
        top = column(top)
        numer = jnp.zeros((HROWS, HD), F32)
        for j, factor in zip(sources, factors):
            numer = numer + column(factor) * got_ref[j, 0:HROWS, :].astype(F32)
        cut = slice(part * HROWS, (part + 1) * HROWS)
        near = peak_ref[cut, :]
        big = jnp.maximum(top, near)
        far_weight = jnp.exp2((top - big) * LOG2E)
        near_weight = jnp.exp2((near - big) * LOG2E)
        result = (numer * far_weight + acc_ref[cut, :] * near_weight) / (
            denom * far_weight + total_ref[cut, :] * near_weight
        )
        for h in range(HROWS // STEPS):
            at = part * (HROWS // STEPS) + h
            out_ref[0, :, at * HD : (at + 1) * HD] = result[h * STEPS : (h + 1) * STEPS].astype(BF16)


def combine(got, acc, peak, total):
    vmem = pl.BlockSpec(memory_space=pltpu.VMEM)
    return pl.pallas_call(
        combine_kernel,
        out_shape=jax.ShapeDtypeStruct((1, STEPS, QH * HD), BF16),
        in_specs=[vmem] * 4,
        out_specs=vmem,
        compiler_params=pltpu.CompilerParams(vmem_limit_bytes=8 << 20),
        name="combine",
    )(got, acc, peak, total)


def local(
    prefix_latent,
    block_order,
    key_up,
    value_up,
    queries,
    new_keys,
    new_values,
    suffix_keys,
    suffix_values,
    suffix_len,
):
    count = lax.axis_size("seq")
    prefix = prefix_latent.shape[0] * count
    core = (lax.axis_index("seq") % 2).astype(jnp.int32)[None]
    swap = [(i, i ^ 1) for i in range(count)]
    send, own, new_rot = rotate_queries(queries, new_keys, suffix_len, prefix, count)
    other_latent = lax.ppermute(prefix_latent, "seq", swap)
    other_order = lax.ppermute(block_order, "seq", swap)
    send, other_order = lax.optimization_barrier((send, other_order))
    gathered = lax.all_to_all(send, "seq", split_axis=0, concat_axis=0, tiled=True)
    keys, values = project(core, block_order, other_order, prefix_latent, other_latent, key_up, value_up)
    parts = attend(gathered, keys, values)
    got = lax.all_to_all(parts, "seq", split_axis=0, concat_axis=0, tiled=True)
    new_pad = jnp.pad(new_values[0], ((0, 16 - STEPS), (0, 0)))
    acc, peak, total = suffix(suffix_len, own, new_rot, new_pad, suffix_keys, suffix_values)
    return combine(got, acc, peak, total)


def solution(mesh):
    placed = (
        P(("parts", "seq"), None),
        P(("parts", "seq")),
        P(),
        P(),
        P(("parts", "seq"), None, None),
        P(("parts", "seq"), None, None),
        P(("parts", "seq"), None, None),
        P(("parts", "seq"), None, None),
        P(("parts", "seq"), None, None),
        P(("parts", "seq")),
    )
    return jax.shard_map(
        local,
        mesh=mesh,
        in_specs=placed,
        out_specs=P(("parts", "seq"), None, None),
        check_vma=False,
    )
```

```python
import functools
import math

import jax
import jax.numpy as jnp
import numpy as np
from jax import lax
from jax.experimental import pallas as pl
from jax.experimental.pallas import tpu as pltpu
from jax.sharding import PartitionSpec as P

HD = 128
QH = 32
KVH = 4
BLK = 128
STEPS = 4
SUF = 4096
GROUP = QH // KVH
HALF_KV = KVH // 2
WIDE = HALF_KV * HD
KROWS = GROUP * STEPS
HROWS = HALF_KV * KROWS
ROWS = KVH * KROWS
PAY = HROWS + 8
SCALE = 1.0 / math.sqrt(HD)
EXP2 = SCALE * math.log2(math.e)
TURN = 2.0 * math.pi / 16777216.0
SUF_TILE = 1024
PER = 15
Q_GROUP = 16
CHUNKS = 5
F32 = jnp.float32
BF16 = jnp.bfloat16


def multipliers():
    half = HD // 2
    index = np.arange(half)
    freq = 500000.0 ** (-2.0 * index / (2 * half))
    return np.floor(2.0**24 * freq / (2 * np.pi)).astype(np.int64)


def phase_rows():
    mult = np.tile(multipliers(), 2)
    table = np.zeros((8, HD), np.int32)
    table[0] = mult >> 12
    table[1] = mult & 4095
    return table


def row_tables():
    mult = np.tile(multipliers(), 2)
    turns = (np.arange(BLK)[:, None] * mult[None, :]) % 16777216
    angle = turns * (2.0 * np.pi / 16777216.0)
    sign = np.where(np.arange(HD) < HD // 2, -1.0, 1.0)
    return (np.cos(angle).astype(np.float32), (np.sin(angle) * sign).astype(np.float32))


def phases(spot, high, low):
    first = spot * low
    second = (spot * high) & 4095
    turns = (first + second * 4096) & 16777215
    return turns.astype(F32) * TURN


def lane_sign(shape):
    lane = lax.broadcasted_iota(jnp.int32, shape, len(shape) - 1)
    return jnp.where(lane < HD // 2, -1.0, 1.0).astype(F32)


def turn(x, cosine, sine):
    return x * cosine + pltpu.roll(x, HD // 2, axis=1) * sine


def query_kernel(prefix, count, len_ref, table_ref, q_ref, nk_ref, send_ref, own_ref, new_ref, rows_ref, nrows_ref):
    step = lax.broadcasted_iota(jnp.int32, (8, HD), 0) % STEPS
    spot = prefix + jnp.broadcast_to(len_ref[...][None], (8, HD)) + step
    angle = phases(spot, table_ref[0:1, :], table_ref[1:2, :])
    cosine = jnp.cos(angle)
    sine = jnp.sin(angle) * lane_sign((8, HD))
    q = q_ref[0].astype(F32)
    for h in range(QH):
        rows_ref[h * STEPS : (h + 1) * STEPS, :] = q[:, h * HD : (h + 1) * HD]
    for i in range(ROWS // 8):
        rows_ref[i * 8 : i * 8 + 8, :] = turn(rows_ref[i * 8 : i * 8 + 8, :], cosine, sine)
    rotated = rows_ref[...].astype(BF16)
    own_ref[...] = rotated
    for d in range(count):
        part = d % 2
        send_ref[d] = rotated[part * HROWS : (part + 1) * HROWS]
    nrows_ref[...] = jnp.zeros_like(nrows_ref)
    nk = nk_ref[0].astype(F32)
    for k in range(KVH):
        cut = slice(k * HD, (k + 1) * HD)
        nrows_ref[0:STEPS, cut] = turn(nk[:, cut], cosine[0:STEPS], sine[0:STEPS])
    new_ref[...] = nrows_ref[...].astype(BF16)


def rotate_queries(queries, new_keys, suffix_len, prefix, count):
    vmem = pl.BlockSpec(memory_space=pltpu.VMEM)
    return pl.pallas_call(
        functools.partial(query_kernel, prefix, count),
        out_shape=(
            jax.ShapeDtypeStruct((count, HROWS, HD), BF16),
            jax.ShapeDtypeStruct((ROWS, HD), BF16),
            jax.ShapeDtypeStruct((16, KVH * HD), BF16),
        ),
        in_specs=[vmem] * 4,
        out_specs=(vmem, vmem, vmem),
        scratch_shapes=[pltpu.VMEM((ROWS, HD), F32), pltpu.VMEM((16, KVH * HD), F32)],
        name="rotate_queries",
    )(suffix_len, jnp.asarray(phase_rows()), queries, new_keys)


def project_kernel(
    core_ref,
    order0_ref,
    order1_ref,
    lat0_hbm,
    lat1_hbm,
    ku_hbm,
    vu_hbm,
    table_ref,
    rc_ref,
    rs_ref,
    k0_ref,
    v0_hbm,
    k_hbm,
    v_hbm,
    bc_ref,
    bs_ref,
    lat_ref,
    w_ref,
    v0_ref,
    k_ref,
    v_ref,
    in_sem,
    w_sem,
    out_sem,
):
    pre_rows = lat0_hbm.shape[0]
    blocks = pre_rows // BLK
    per = max(d for d in range(1, PER + 1) if blocks % d == 0)
    chunks = blocks // per
    size = per * BLK
    mine = pl.ds(pl.multiple_of(core_ref[0] * WIDE, WIDE), WIDE)
    loads = [
        pltpu.make_async_copy(ku_hbm.at[:, mine], w_ref.at[:, 0:WIDE], w_sem.at[0]),
        pltpu.make_async_copy(vu_hbm.at[:, mine], w_ref.at[:, WIDE : 2 * WIDE], w_sem.at[1]),
    ]
    fetches = []
    for side, source in enumerate((lat0_hbm, lat1_hbm)):
        for c in range(chunks):
            at = pl.ds(c * size, size)
            slot = side * chunks + c
            fetches.append(pltpu.make_async_copy(source.at[at], lat_ref.at[pl.ds(slot * size, size)], in_sem.at[slot]))
    loads[0].start()
    fetches[0].start()
    loads[1].start()
    for fetch in fetches[1:]:
        fetch.start()
    pad = bc_ref.shape[0]
    narrow = lax.broadcasted_iota(jnp.int32, (pad, blocks), 1)
    tall = lax.broadcasted_iota(jnp.int32, (pad, blocks), 0)
    spot = jnp.zeros((pad, 1), F32)
    for side, order_ref in enumerate((order0_ref, order1_ref)):
        order = jnp.broadcast_to(order_ref[...].astype(F32), (pad, blocks))
        spot = spot + jnp.sum(jnp.where(tall == side * blocks + narrow, order, 0.0), -1, keepdims=True)
    spot = jnp.broadcast_to(spot.astype(jnp.int32), (pad, HD))
    angle = phases(spot * BLK, table_ref[0:1, :], table_ref[1:2, :])
    bc_ref[...] = jnp.cos(angle)
    bs_ref[...] = jnp.sin(angle) * lane_sign((pad, HD))
    loads[0].wait()
    loads[1].wait()
    stores = []
    for slot in range(2 * chunks):
        at = pl.ds(slot * size, size)
        fetches[slot].wait()
        lat = lat_ref[at, :]
        keys = jnp.dot(lat, w_ref[...], preferred_element_type=F32)
        values = keys[:, WIDE:].astype(BF16)
        for target, k in ((v0_ref, 0), (v_ref, 1)):
            target[at, :] = values[:, k * HD : (k + 1) * HD]
        for i in range(per):
            b = slot * per + i
            block_cos = bc_ref[b : b + 1, :]
            block_sin = bs_ref[b : b + 1, :]
            cosine = block_cos * rc_ref[...] - block_sin * rs_ref[...]
            sine = block_sin * rc_ref[...] + block_cos * rs_ref[...]
            for target, k in ((k0_ref, 0), (k_ref, 1)):
                part = keys[i * BLK : (i + 1) * BLK, k * HD : (k + 1) * HD]
                target[b * BLK : (b + 1) * BLK, :] = turn(part, cosine, sine).astype(BF16)
        for kind, (source, target) in enumerate(((v0_ref, v0_hbm), (k_ref, k_hbm), (v_ref, v_hbm))):
            store = pltpu.make_async_copy(source.at[at], target.at[at], out_sem.at[slot * 3 + kind])
            store.start()
            stores.append(store)
    for store in stores:
        store.wait()


def project(core, order0, order1, latent0, latent1, key_up, value_up):
    pre_rows, rank = latent0.shape
    blocks = pre_rows // BLK
    per = max(d for d in range(1, PER + 1) if blocks % d == 0)
    slots = 2 * blocks // per
    rows = 2 * pre_rows
    rc, rs = row_tables()
    smem = pl.BlockSpec(memory_space=pltpu.SMEM)
    vmem = pl.BlockSpec(memory_space=pltpu.VMEM)
    hbm = pl.BlockSpec(memory_space=pl.ANY)
    pad = -(-2 * blocks // 8) * 8
    out = jax.ShapeDtypeStruct((rows, HD), BF16)
    out_far = pltpu.HBM((rows, HD), BF16)
    return pl.pallas_call(
        project_kernel,
        out_shape=(out, out_far, out_far, out_far),
        in_specs=[smem, vmem, vmem, hbm, hbm, hbm, hbm, vmem, vmem, vmem],
        out_specs=(vmem, hbm, hbm, hbm),
        scratch_shapes=[
            pltpu.VMEM((pad, HD), F32),
            pltpu.VMEM((pad, HD), F32),
            pltpu.VMEM((rows, rank), BF16),
            pltpu.VMEM((rank, 2 * WIDE), BF16),
            pltpu.VMEM((rows, HD), BF16),
            pltpu.VMEM((rows, HD), BF16),
            pltpu.VMEM((rows, HD), BF16),
            pltpu.SemaphoreType.DMA((slots,)),
            pltpu.SemaphoreType.DMA((2,)),
            pltpu.SemaphoreType.DMA((slots * 3,)),
        ],
        cost_estimate=pl.CostEstimate(
            flops=4 * rows * rank * WIDE, bytes_accessed=rows * (rank + 2 * WIDE) * 2, transcendentals=0
        ),
        compiler_params=pltpu.CompilerParams(vmem_limit_bytes=40 << 20),
        name="project",
    )(
        core,
        far(order0[None]),
        order1[None],
        far(latent0),
        latent1,
        far(key_up),
        far(value_up),
        far(jnp.asarray(phase_rows())),
        far(jnp.asarray(rc)),
        far(jnp.asarray(rs)),
    )


def far(x):
    return pltpu.with_memory_space_constraint(x, pltpu.HBM)


def three(x):
    first = x.astype(BF16).astype(F32)
    rest = x - first
    second = rest.astype(BF16).astype(F32)
    return first, second, rest - second


def attend_kernel(per, q_ref, k0_ref, v0_hbm, k_hbm, v_hbm, out_ref, v0_ref, k_ref, v_ref, stat_ref, sem):
    nt = (((1,), (1,)), ((), ()))
    row = lax.broadcasted_iota(jnp.int32, (KROWS, HD), 0)
    lane = lax.broadcasted_iota(jnp.int32, (KROWS, HD), 1)
    place = lax.broadcasted_iota(jnp.int32, (8, HD), 0)
    fetches = [
        pltpu.make_async_copy(v0_hbm, v0_ref, sem.at[0]),
        pltpu.make_async_copy(k_hbm, k_ref, sem.at[1]),
        pltpu.make_async_copy(v_hbm, v_ref, sem.at[2]),
    ]
    for fetch in fetches:
        fetch.start()

    for k in range(HALF_KV):
        if k:
            fetches[1].wait()
            fetches[2].wait()
        keys, values = ((k0_ref, v0_ref), (k_ref, v_ref))[k]

        def group(g, first=False, k=k, keys=keys, values=values):
            base = g * per
            rows = slice(k * KROWS, (k + 1) * KROWS)
            q = q_ref[pl.ds(base, per), rows, :].reshape(per * KROWS, HD)
            width = k_hbm.shape[0] // CHUNKS

            def score(c):
                return lax.dot_general(q, keys[c * width : (c + 1) * width, :], nt, preferred_element_type=F32)

            ahead = score(0)
            for c in range(CHUNKS):
                s = ahead
                if c + 1 < CHUNKS:
                    ahead = score(c + 1)
                best = jnp.max(s, -1, keepdims=True)
                if first and c == 0:
                    fetches[0].wait()
                if c:
                    best = jnp.maximum(peak, best)
                    keep = jnp.exp2((peak - best) * EXP2)
                e = jnp.exp2((s - best) * EXP2)
                here = jnp.sum(e, -1, keepdims=True)
                o = jnp.dot(e.astype(BF16), values[c * width : (c + 1) * width, :], preferred_element_type=F32)
                total = total * keep + here if c else here
                acc = acc * keep + o if c else o
                peak = best
            o = acc / total
            out_ref[pl.ds(base, per), rows, :] = o.astype(BF16).reshape(per, KROWS, HD)
            peak = peak * EXP2
            for r in range(per):
                cut = slice(r * KROWS, (r + 1) * KROWS)
                stats = jnp.zeros((8, HD), F32)
                for i, part in enumerate((peak, total)):
                    spread = jnp.where(lane == row + k * KROWS, part[cut], 0.0)
                    for j, line in enumerate(three(jnp.sum(spread, 0, keepdims=True))):
                        stats = jnp.where(place == 3 * i + j, line, stats)
                if k == 0:
                    stat_ref[base + r] = stats
                else:
                    out_ref[base + r, HROWS:PAY, :] = (stat_ref[base + r] + stats).astype(BF16)

        group(0, k == 0)
        groups = q_ref.shape[0] // per
        if groups > 1:
            pl.loop(1, groups)(group)


def attend(q, k0, v0, k1, v1):
    count = q.shape[0]
    rows = k0.shape[0]
    vmem = pl.BlockSpec(memory_space=pltpu.VMEM)
    hbm = pl.BlockSpec(memory_space=pl.ANY)
    return pl.pallas_call(
        functools.partial(attend_kernel, math.gcd(count, Q_GROUP)),
        out_shape=jax.ShapeDtypeStruct((count, PAY, HD), BF16),
        in_specs=[vmem, vmem, hbm, hbm, hbm],
        out_specs=vmem,
        scratch_shapes=[
            pltpu.VMEM((rows, HD), BF16),
            pltpu.VMEM((rows, HD), BF16),
            pltpu.VMEM((rows, HD), BF16),
            pltpu.VMEM((count, 8, HD), F32),
            pltpu.SemaphoreType.DMA((3,)),
        ],
        compiler_params=pltpu.CompilerParams(vmem_limit_bytes=48 << 20),
        cost_estimate=pl.CostEstimate(
            flops=4 * count * HROWS * HD * rows,
            bytes_accessed=4 * rows * WIDE,
            transcendentals=count * HROWS * rows,
        ),
        name="attend",
    )(q, k0, far(v0), far(k1), far(v1))


def suffix_kernel(len_ref, q_ref, nk_ref, nv_ref, k_ref, v_ref, acc_ref, peak_ref, total_ref):
    step = pl.program_id(0)
    length = len_ref[0]
    tile = k_ref.shape[1]
    nt = (((1,), (1,)), ((), ()))

    def scores(keys):
        return jnp.concatenate(
            [
                lax.dot_general(
                    q_ref[k * KROWS : (k + 1) * KROWS, :],
                    keys[:, k * HD : (k + 1) * HD],
                    nt,
                    preferred_element_type=F32,
                )
                for k in range(KVH)
            ],
            0,
        )

    def weigh(probs, values):
        probs = probs.astype(BF16)
        return jnp.concatenate(
            [
                jnp.dot(
                    probs[k * KROWS : (k + 1) * KROWS],
                    values[:, k * HD : (k + 1) * HD],
                    preferred_element_type=F32,
                )
                for k in range(KVH)
            ],
            0,
        )

    @pl.when(step == 0)
    def _():
        s = scores(nk_ref[...])
        row = lax.broadcasted_iota(jnp.int32, s.shape, 0) % STEPS
        lane = lax.broadcasted_iota(jnp.int32, s.shape, 1)
        s = jnp.where(lane <= row, s, -jnp.inf)
        peak = jnp.max(s, -1, keepdims=True)
        e = jnp.exp2((s - peak) * EXP2)
        acc_ref[...] = weigh(e, nv_ref[...])
        peak_ref[...] = jnp.broadcast_to(peak, peak_ref.shape)
        total_ref[...] = jnp.broadcast_to(jnp.sum(e, -1, keepdims=True), total_ref.shape)

    @pl.when(step * tile < length)
    def _():
        s = scores(k_ref[0])
        spot = step * tile + lax.broadcasted_iota(jnp.int32, s.shape, 1)
        s = jnp.where(spot < length, s, -jnp.inf)
        old = peak_ref[:, 0:1]
        peak = jnp.maximum(old, jnp.max(s, -1, keepdims=True))
        keep = jnp.exp2((old - peak) * EXP2)
        e = jnp.exp2((s - peak) * EXP2)
        acc_ref[...] = acc_ref[...] * keep + weigh(e, v_ref[0])
        total_ref[...] = total_ref[...] * keep + jnp.sum(e, -1, keepdims=True)
        peak_ref[...] = jnp.broadcast_to(peak, peak_ref.shape)

    @pl.when(step == pl.num_programs(0) - 1)
    def _():
        peak_ref[...] = peak_ref[...] * EXP2


def suffix(length, q, new_rot, new_values, keys, values):
    tile = SUF_TILE
    fixed = lambda i, n: (0, 0)
    walk = lambda i, n: (0, jnp.minimum(i, (n[0] - 1) // tile), 0)
    out = jax.ShapeDtypeStruct((ROWS, HD), F32)
    return pl.pallas_call(
        suffix_kernel,
        out_shape=(out, out, out),
        grid_spec=pltpu.PrefetchScalarGridSpec(
            num_scalar_prefetch=1,
            grid=(SUF // tile,),
            in_specs=[
                pl.BlockSpec((ROWS, HD), fixed),
                pl.BlockSpec((16, KVH * HD), fixed),
                pl.BlockSpec((16, KVH * HD), fixed),
                pl.BlockSpec((1, tile, KVH * HD), walk),
                pl.BlockSpec((1, tile, KVH * HD), walk),
            ],
            out_specs=[pl.BlockSpec((ROWS, HD), fixed)] * 3,
        ),
        cost_estimate=pl.CostEstimate(
            flops=4 * ROWS * SUF * HD, bytes_accessed=4 * SUF * KVH * HD, transcendentals=ROWS * SUF
        ),
        compiler_params=pltpu.CompilerParams(vmem_limit_bytes=40 << 20),
        name="suffix",
    )(length, q, new_rot, new_values, far(keys), far(values))


def combine_kernel(got_ref, acc_ref, peak_ref, total_ref, out_ref):
    count = got_ref.shape[0]
    row = lax.broadcasted_iota(jnp.int32, (HROWS, HD), 0)
    lane = lax.broadcasted_iota(jnp.int32, (HROWS, HD), 1)
    eye = row == lane

    def column(line):
        return jnp.sum(jnp.where(eye, line, 0.0), -1, keepdims=True)

    for part in range(2):
        sources = range(part, count, 2)
        stats = [got_ref[j, HROWS:PAY, :].astype(F32) for j in sources]
        peaks = [s[0:1] + s[1:2] + s[2:3] for s in stats]
        totals = [s[3:4] + s[4:5] + s[5:6] for s in stats]
        top = functools.reduce(jnp.maximum, peaks)
        factors = [t * jnp.exp2(p - top) for p, t in zip(peaks, totals)]
        denom = column(sum(factors))
        top = column(top)
        numer = jnp.zeros((HROWS, HD), F32)
        for j, factor in zip(sources, factors):
            numer = numer + column(factor) * got_ref[j, 0:HROWS, :].astype(F32)
        cut = slice(part * HROWS, (part + 1) * HROWS)
        near = peak_ref[cut, :]
        big = jnp.maximum(top, near)
        far_weight = jnp.exp2(top - big)
        near_weight = jnp.exp2(near - big)
        result = (numer * far_weight + acc_ref[cut, :] * near_weight) / (
            denom * far_weight + total_ref[cut, :] * near_weight
        )
        for h in range(HROWS // STEPS):
            at = part * (HROWS // STEPS) + h
            out_ref[0, :, at * HD : (at + 1) * HD] = result[h * STEPS : (h + 1) * STEPS].astype(BF16)


def combine(got, acc, peak, total):
    vmem = pl.BlockSpec(memory_space=pltpu.VMEM)
    return pl.pallas_call(
        combine_kernel,
        out_shape=jax.ShapeDtypeStruct((1, STEPS, QH * HD), BF16),
        in_specs=[vmem] * 4,
        out_specs=vmem,
        compiler_params=pltpu.CompilerParams(vmem_limit_bytes=8 << 20),
        name="combine",
    )(got, acc, peak, total)


def local(
    prefix_latent,
    block_order,
    key_up,
    value_up,
    queries,
    new_keys,
    new_values,
    suffix_keys,
    suffix_values,
    suffix_len,
):
    count = lax.axis_size("seq")
    prefix = prefix_latent.shape[0] * count
    core = (lax.axis_index("seq") % 2).astype(jnp.int32)[None]
    swap = [(i, i ^ 1) for i in range(count)]
    send, own, new_rot = rotate_queries(queries, new_keys, suffix_len, prefix, count)
    other_latent = lax.ppermute(prefix_latent, "seq", swap)
    other_order = lax.ppermute(block_order, "seq", swap)
    gathered = lax.all_to_all(send, "seq", split_axis=0, concat_axis=0, tiled=True)
    projected = project(core, block_order, other_order, prefix_latent, other_latent, key_up, value_up)
    parts = attend(gathered, *projected)
    got = lax.all_to_all(parts, "seq", split_axis=0, concat_axis=0, tiled=True)
    new_pad = jnp.pad(new_values[0], ((0, 16 - STEPS), (0, 0)))
    acc, peak, total = suffix(suffix_len, own, new_rot, new_pad, suffix_keys, suffix_values)
    return combine(got, acc, peak, total)


def solution(mesh):
    placed = (
        P(("parts", "seq"), None),
        P(("parts", "seq")),
        P(),
        P(),
        P(("parts", "seq"), None, None),
        P(("parts", "seq"), None, None),
        P(("parts", "seq"), None, None),
        P(("parts", "seq"), None, None),
        P(("parts", "seq"), None, None),
        P(("parts", "seq")),
    )
    return jax.shard_map(
        local,
        mesh=mesh,
        in_specs=placed,
        out_specs=P(("parts", "seq"), None, None),
        check_vma=False,
    )
```

```python
import functools
import math

import jax
import jax.numpy as jnp
import numpy as np
from jax import lax
from jax.experimental import pallas as pl
from jax.experimental.pallas import tpu as pltpu
from jax.sharding import PartitionSpec as P

HD = 128
QH = 32
KVH = 4
BLK = 128
STEPS = 4
SUF = 4096
GROUP = QH // KVH
HALF_KV = KVH // 2
WIDE = HALF_KV * HD
KROWS = GROUP * STEPS
HROWS = HALF_KV * KROWS
ROWS = KVH * KROWS
PAY = HROWS + 8
SCALE = 1.0 / math.sqrt(HD)
EXP2 = SCALE * math.log2(math.e)
TURN = 2.0 * math.pi / 16777216.0
SUF_TILE = 1024
PER = 15
Q_GROUP = 16
CHUNKS = 5
F32 = jnp.float32
BF16 = jnp.bfloat16


def multipliers():
    half = HD // 2
    index = np.arange(half)
    freq = 500000.0 ** (-2.0 * index / (2 * half))
    return np.floor(2.0**24 * freq / (2 * np.pi)).astype(np.int64)


def phase_rows():
    mult = np.tile(multipliers(), 2)
    table = np.zeros((8, HD), np.int32)
    table[0] = mult >> 12
    table[1] = mult & 4095
    return table


def row_tables():
    mult = np.tile(multipliers(), 2)
    turns = (np.arange(BLK)[:, None] * mult[None, :]) % 16777216
    angle = turns * (2.0 * np.pi / 16777216.0)
    sign = np.where(np.arange(HD) < HD // 2, -1.0, 1.0)
    return (np.cos(angle).astype(np.float32), (np.sin(angle) * sign).astype(np.float32))


def phases(spot, high, low):
    first = spot * low
    second = (spot * high) & 4095
    turns = (first + second * 4096) & 16777215
    return turns.astype(F32) * TURN


def lane_sign(shape):
    lane = lax.broadcasted_iota(jnp.int32, shape, len(shape) - 1)
    return jnp.where(lane < HD // 2, -1.0, 1.0).astype(F32)


def turn(x, cosine, sine):
    return x * cosine + pltpu.roll(x, HD // 2, axis=1) * sine


def query_kernel(prefix, count, len_ref, table_ref, q_ref, nk_ref, send_ref, own_ref, new_ref, rows_ref, nrows_ref):
    step = lax.broadcasted_iota(jnp.int32, (8, HD), 0) % STEPS
    spot = prefix + jnp.broadcast_to(len_ref[...][None], (8, HD)) + step
    angle = phases(spot, table_ref[0:1, :], table_ref[1:2, :])
    cosine = jnp.cos(angle)
    sine = jnp.sin(angle) * lane_sign((8, HD))
    q = q_ref[0].astype(F32)
    for h in range(QH):
        rows_ref[h * STEPS : (h + 1) * STEPS, :] = q[:, h * HD : (h + 1) * HD]
    for i in range(ROWS // 8):
        rows_ref[i * 8 : i * 8 + 8, :] = turn(rows_ref[i * 8 : i * 8 + 8, :], cosine, sine)
    rotated = rows_ref[...].astype(BF16)
    own_ref[...] = rotated
    for d in range(count):
        part = d % 2
        send_ref[d] = rotated[part * HROWS : (part + 1) * HROWS]
    nrows_ref[...] = jnp.zeros_like(nrows_ref)
    nk = nk_ref[0].astype(F32)
    for k in range(KVH):
        cut = slice(k * HD, (k + 1) * HD)
        nrows_ref[0:STEPS, cut] = turn(nk[:, cut], cosine[0:STEPS], sine[0:STEPS])
    new_ref[...] = nrows_ref[...].astype(BF16)


def rotate_queries(queries, new_keys, suffix_len, prefix, count):
    vmem = pl.BlockSpec(memory_space=pltpu.VMEM)
    return pl.pallas_call(
        functools.partial(query_kernel, prefix, count),
        out_shape=(
            jax.ShapeDtypeStruct((count, HROWS, HD), BF16),
            jax.ShapeDtypeStruct((ROWS, HD), BF16),
            jax.ShapeDtypeStruct((16, KVH * HD), BF16),
        ),
        in_specs=[vmem] * 4,
        out_specs=(vmem, vmem, vmem),
        scratch_shapes=[pltpu.VMEM((ROWS, HD), F32), pltpu.VMEM((16, KVH * HD), F32)],
        name="rotate_queries",
    )(suffix_len, jnp.asarray(phase_rows()), queries, new_keys)


def project_kernel(
    core_ref,
    order0_ref,
    order1_ref,
    lat0_hbm,
    lat1_hbm,
    ku_hbm,
    vu_hbm,
    table_ref,
    rc_ref,
    rs_ref,
    k0_ref,
    v0_hbm,
    k_hbm,
    v_hbm,
    bc_ref,
    bs_ref,
    lat_ref,
    w_ref,
    v0_ref,
    k_ref,
    v_ref,
    in_sem,
    w_sem,
    out_sem,
):
    pre_rows = lat0_hbm.shape[0]
    blocks = pre_rows // BLK
    per = max(d for d in range(1, PER + 1) if blocks % d == 0)
    chunks = blocks // per
    size = per * BLK
    mine = pl.ds(pl.multiple_of(core_ref[0] * WIDE, WIDE), WIDE)
    loads = [
        pltpu.make_async_copy(ku_hbm.at[:, mine], w_ref.at[:, 0:WIDE], w_sem.at[0]),
        pltpu.make_async_copy(vu_hbm.at[:, mine], w_ref.at[:, WIDE : 2 * WIDE], w_sem.at[1]),
    ]
    fetches = []
    for side, source in enumerate((lat0_hbm, lat1_hbm)):
        for c in range(chunks):
            at = pl.ds(c * size, size)
            slot = side * chunks + c
            fetches.append(pltpu.make_async_copy(source.at[at], lat_ref.at[pl.ds(slot * size, size)], in_sem.at[slot]))
    loads[0].start()
    fetches[0].start()
    loads[1].start()
    for fetch in fetches[1:]:
        fetch.start()
    pad = bc_ref.shape[0]
    narrow = lax.broadcasted_iota(jnp.int32, (pad, blocks), 1)
    tall = lax.broadcasted_iota(jnp.int32, (pad, blocks), 0)
    spot = jnp.zeros((pad, 1), F32)
    for side, order_ref in enumerate((order0_ref, order1_ref)):
        order = jnp.broadcast_to(order_ref[...].astype(F32), (pad, blocks))
        spot = spot + jnp.sum(jnp.where(tall == side * blocks + narrow, order, 0.0), -1, keepdims=True)
    spot = jnp.broadcast_to(spot.astype(jnp.int32), (pad, HD))
    angle = phases(spot * BLK, table_ref[0:1, :], table_ref[1:2, :])
    bc_ref[...] = jnp.cos(angle)
    bs_ref[...] = jnp.sin(angle) * lane_sign((pad, HD))
    loads[0].wait()
    loads[1].wait()
    stores = []
    for slot in range(2 * chunks):
        at = pl.ds(slot * size, size)
        fetches[slot].wait()
        lat = lat_ref[at, :]
        keys = jnp.dot(lat, w_ref[...], preferred_element_type=F32)
        values = keys[:, WIDE:].astype(BF16)
        for target, k in ((v0_ref, 0), (v_ref, 1)):
            target[at, :] = values[:, k * HD : (k + 1) * HD]
        for i in range(per):
            b = slot * per + i
            block_cos = bc_ref[b : b + 1, :]
            block_sin = bs_ref[b : b + 1, :]
            cosine = block_cos * rc_ref[...] - block_sin * rs_ref[...]
            sine = block_sin * rc_ref[...] + block_cos * rs_ref[...]
            for target, k in ((k0_ref, 0), (k_ref, 1)):
                part = keys[i * BLK : (i + 1) * BLK, k * HD : (k + 1) * HD]
                target[b * BLK : (b + 1) * BLK, :] = turn(part, cosine, sine).astype(BF16)
        for kind, (source, target) in enumerate(((v0_ref, v0_hbm), (k_ref, k_hbm), (v_ref, v_hbm))):
            store = pltpu.make_async_copy(source.at[at], target.at[at], out_sem.at[slot * 3 + kind])
            store.start()
            stores.append(store)
    for store in stores:
        store.wait()


def project(core, order0, order1, latent0, latent1, key_up, value_up):
    pre_rows, rank = latent0.shape
    blocks = pre_rows // BLK
    per = max(d for d in range(1, PER + 1) if blocks % d == 0)
    slots = 2 * blocks // per
    rows = 2 * pre_rows
    rc, rs = row_tables()
    smem = pl.BlockSpec(memory_space=pltpu.SMEM)
    vmem = pl.BlockSpec(memory_space=pltpu.VMEM)
    hbm = pl.BlockSpec(memory_space=pl.ANY)
    pad = -(-2 * blocks // 8) * 8
    out = jax.ShapeDtypeStruct((rows, HD), BF16)
    out_far = pltpu.HBM((rows, HD), BF16)
    return pl.pallas_call(
        project_kernel,
        out_shape=(out, out_far, out_far, out_far),
        in_specs=[smem, vmem, vmem, hbm, hbm, hbm, hbm, vmem, vmem, vmem],
        out_specs=(vmem, hbm, hbm, hbm),
        scratch_shapes=[
            pltpu.VMEM((pad, HD), F32),
            pltpu.VMEM((pad, HD), F32),
            pltpu.VMEM((rows, rank), BF16),
            pltpu.VMEM((rank, 2 * WIDE), BF16),
            pltpu.VMEM((rows, HD), BF16),
            pltpu.VMEM((rows, HD), BF16),
            pltpu.VMEM((rows, HD), BF16),
            pltpu.SemaphoreType.DMA((slots,)),
            pltpu.SemaphoreType.DMA((2,)),
            pltpu.SemaphoreType.DMA((slots * 3,)),
        ],
        cost_estimate=pl.CostEstimate(
            flops=4 * rows * rank * WIDE, bytes_accessed=rows * (rank + 2 * WIDE) * 2, transcendentals=0
        ),
        compiler_params=pltpu.CompilerParams(vmem_limit_bytes=40 << 20),
        name="project",
    )(
        core,
        far(order0[None]),
        order1[None],
        far(latent0),
        latent1,
        far(key_up),
        far(value_up),
        far(jnp.asarray(phase_rows())),
        far(jnp.asarray(rc)),
        far(jnp.asarray(rs)),
    )


def far(x):
    return pltpu.with_memory_space_constraint(x, pltpu.HBM)


def three(x):
    first = x.astype(BF16).astype(F32)
    rest = x - first
    second = rest.astype(BF16).astype(F32)
    return first, second, rest - second


def attend_kernel(per, q_ref, k0_ref, v0_hbm, k_hbm, v_hbm, out_ref, v0_ref, k_ref, v_ref, stat_ref, sem):
    nt = (((1,), (1,)), ((), ()))
    row = lax.broadcasted_iota(jnp.int32, (KROWS, HD), 0)
    lane = lax.broadcasted_iota(jnp.int32, (KROWS, HD), 1)
    place = lax.broadcasted_iota(jnp.int32, (8, HD), 0)
    fetches = [
        pltpu.make_async_copy(v0_hbm, v0_ref, sem.at[0]),
        pltpu.make_async_copy(k_hbm, k_ref, sem.at[1]),
        pltpu.make_async_copy(v_hbm, v_ref, sem.at[2]),
    ]
    for fetch in fetches:
        fetch.start()

    for k in range(HALF_KV):
        if k:
            fetches[1].wait()
            fetches[2].wait()
        keys, values = ((k0_ref, v0_ref), (k_ref, v_ref))[k]

        def group(g, first=False, k=k, keys=keys, values=values):
            base = g * per
            rows = slice(k * KROWS, (k + 1) * KROWS)
            q = q_ref[pl.ds(base, per), rows, :].reshape(per * KROWS, HD)
            width = k_hbm.shape[0] // CHUNKS

            def score(c):
                return lax.dot_general(q, keys[c * width : (c + 1) * width, :], nt, preferred_element_type=F32)

            ahead = score(0)
            for c in range(CHUNKS):
                s = ahead
                if c + 1 < CHUNKS:
                    ahead = score(c + 1)
                best = jnp.max(s, -1, keepdims=True)
                if first and c == 0:
                    fetches[0].wait()
                if c:
                    best = jnp.maximum(peak, best)
                    keep = jnp.exp2((peak - best) * EXP2)
                e = jnp.exp2((s - best) * EXP2)
                here = jnp.sum(e, -1, keepdims=True)
                o = jnp.dot(e.astype(BF16), values[c * width : (c + 1) * width, :], preferred_element_type=F32)
                total = total * keep + here if c else here
                acc = acc * keep + o if c else o
                peak = best
            o = acc / total
            out_ref[pl.ds(base, per), rows, :] = o.astype(BF16).reshape(per, KROWS, HD)
            peak = peak * EXP2
            for r in range(per):
                cut = slice(r * KROWS, (r + 1) * KROWS)
                stats = jnp.zeros((8, HD), F32)
                for i, part in enumerate((peak, total)):
                    spread = jnp.where(lane == row + k * KROWS, part[cut], 0.0)
                    for j, line in enumerate(three(jnp.sum(spread, 0, keepdims=True))):
                        stats = jnp.where(place == 3 * i + j, line, stats)
                if k == 0:
                    stat_ref[base + r] = stats
                else:
                    out_ref[base + r, HROWS:PAY, :] = (stat_ref[base + r] + stats).astype(BF16)

        group(0, k == 0)
        groups = q_ref.shape[0] // per
        if groups > 1:
            pl.loop(1, groups)(group)


def attend(q, k0, v0, k1, v1):
    count = q.shape[0]
    rows = k0.shape[0]
    vmem = pl.BlockSpec(memory_space=pltpu.VMEM)
    hbm = pl.BlockSpec(memory_space=pl.ANY)
    return pl.pallas_call(
        functools.partial(attend_kernel, math.gcd(count, Q_GROUP)),
        out_shape=jax.ShapeDtypeStruct((count, PAY, HD), BF16),
        in_specs=[vmem, vmem, hbm, hbm, hbm],
        out_specs=vmem,
        scratch_shapes=[
            pltpu.VMEM((rows, HD), BF16),
            pltpu.VMEM((rows, HD), BF16),
            pltpu.VMEM((rows, HD), BF16),
            pltpu.VMEM((count, 8, HD), F32),
            pltpu.SemaphoreType.DMA((3,)),
        ],
        compiler_params=pltpu.CompilerParams(vmem_limit_bytes=48 << 20),
        cost_estimate=pl.CostEstimate(
            flops=4 * count * HROWS * HD * rows,
            bytes_accessed=4 * rows * WIDE,
            transcendentals=count * HROWS * rows,
        ),
        name="attend",
    )(q, k0, far(v0), far(k1), far(v1))


def suffix_kernel(len_ref, q_ref, nk_ref, nv_ref, k_ref, v_ref, acc_ref, peak_ref, total_ref):
    step = pl.program_id(0)
    length = len_ref[0]
    tile = k_ref.shape[1]
    nt = (((1,), (1,)), ((), ()))

    def scores(keys):
        return jnp.concatenate(
            [
                lax.dot_general(
                    q_ref[k * KROWS : (k + 1) * KROWS, :],
                    keys[:, k * HD : (k + 1) * HD],
                    nt,
                    preferred_element_type=F32,
                )
                for k in range(KVH)
            ],
            0,
        )

    def weigh(probs, values):
        probs = probs.astype(BF16)
        return jnp.concatenate(
            [
                jnp.dot(
                    probs[k * KROWS : (k + 1) * KROWS],
                    values[:, k * HD : (k + 1) * HD],
                    preferred_element_type=F32,
                )
                for k in range(KVH)
            ],
            0,
        )

    @pl.when(step == 0)
    def _():
        s = scores(nk_ref[...])
        row = lax.broadcasted_iota(jnp.int32, s.shape, 0) % STEPS
        lane = lax.broadcasted_iota(jnp.int32, s.shape, 1)
        s = jnp.where(lane <= row, s, -jnp.inf)
        peak = jnp.max(s, -1, keepdims=True)
        e = jnp.exp2((s - peak) * EXP2)
        acc_ref[...] = weigh(e, nv_ref[...])
        peak_ref[...] = jnp.broadcast_to(peak, peak_ref.shape)
        total_ref[...] = jnp.broadcast_to(jnp.sum(e, -1, keepdims=True), total_ref.shape)

    @pl.when(step * tile < length)
    def _():
        s = scores(k_ref[0])
        spot = step * tile + lax.broadcasted_iota(jnp.int32, s.shape, 1)
        s = jnp.where(spot < length, s, -jnp.inf)
        old = peak_ref[:, 0:1]
        peak = jnp.maximum(old, jnp.max(s, -1, keepdims=True))
        keep = jnp.exp2((old - peak) * EXP2)
        e = jnp.exp2((s - peak) * EXP2)
        acc_ref[...] = acc_ref[...] * keep + weigh(e, v_ref[0])
        total_ref[...] = total_ref[...] * keep + jnp.sum(e, -1, keepdims=True)
        peak_ref[...] = jnp.broadcast_to(peak, peak_ref.shape)

    @pl.when(step == pl.num_programs(0) - 1)
    def _():
        peak_ref[...] = peak_ref[...] * EXP2


def suffix(length, q, new_rot, new_values, keys, values):
    tile = SUF_TILE
    fixed = lambda i, n: (0, 0)
    walk = lambda i, n: (0, jnp.minimum(i, (n[0] - 1) // tile), 0)
    out = jax.ShapeDtypeStruct((ROWS, HD), F32)
    return pl.pallas_call(
        suffix_kernel,
        out_shape=(out, out, out),
        grid_spec=pltpu.PrefetchScalarGridSpec(
            num_scalar_prefetch=1,
            grid=(SUF // tile,),
            in_specs=[
                pl.BlockSpec((ROWS, HD), fixed),
                pl.BlockSpec((16, KVH * HD), fixed),
                pl.BlockSpec((16, KVH * HD), fixed),
                pl.BlockSpec((1, tile, KVH * HD), walk),
                pl.BlockSpec((1, tile, KVH * HD), walk),
            ],
            out_specs=[pl.BlockSpec((ROWS, HD), fixed)] * 3,
        ),
        cost_estimate=pl.CostEstimate(
            flops=4 * ROWS * SUF * HD, bytes_accessed=4 * SUF * KVH * HD, transcendentals=ROWS * SUF
        ),
        compiler_params=pltpu.CompilerParams(vmem_limit_bytes=40 << 20),
        name="suffix",
    )(length, q, new_rot, new_values, far(keys), far(values))


def combine_kernel(got_ref, acc_ref, peak_ref, total_ref, out_ref):
    count = got_ref.shape[0]
    row = lax.broadcasted_iota(jnp.int32, (HROWS, HD), 0)
    lane = lax.broadcasted_iota(jnp.int32, (HROWS, HD), 1)
    eye = row == lane

    def column(line):
        return jnp.sum(jnp.where(eye, line, 0.0), -1, keepdims=True)

    for part in range(2):
        sources = range(part, count, 2)
        stats = [got_ref[j, HROWS:PAY, :].astype(F32) for j in sources]
        peaks = [s[0:1] + s[1:2] + s[2:3] for s in stats]
        totals = [s[3:4] + s[4:5] + s[5:6] for s in stats]
        top = functools.reduce(jnp.maximum, peaks)
        factors = [t * jnp.exp2(p - top) for p, t in zip(peaks, totals)]
        denom = column(sum(factors))
        top = column(top)
        numer = jnp.zeros((HROWS, HD), F32)
        for j, factor in zip(sources, factors):
            numer = numer + column(factor) * got_ref[j, 0:HROWS, :].astype(F32)
        cut = slice(part * HROWS, (part + 1) * HROWS)
        near = peak_ref[cut, :]
        big = jnp.maximum(top, near)
        far_weight = jnp.exp2(top - big)
        near_weight = jnp.exp2(near - big)
        result = (numer * far_weight + acc_ref[cut, :] * near_weight) / (
            denom * far_weight + total_ref[cut, :] * near_weight
        )
        for h in range(HROWS // STEPS):
            at = part * (HROWS // STEPS) + h
            out_ref[0, :, at * HD : (at + 1) * HD] = result[h * STEPS : (h + 1) * STEPS].astype(BF16)


def combine(got, acc, peak, total):
    vmem = pl.BlockSpec(memory_space=pltpu.VMEM)
    return pl.pallas_call(
        combine_kernel,
        out_shape=jax.ShapeDtypeStruct((1, STEPS, QH * HD), BF16),
        in_specs=[vmem] * 4,
        out_specs=vmem,
        compiler_params=pltpu.CompilerParams(vmem_limit_bytes=8 << 20),
        name="combine",
    )(got, acc, peak, total)


def exchange_order(count):
    chips = count // 2
    middle = chips // 2 / 2 - 0.4
    order = sorted(range(chips), key=lambda chip: (1 - chip % 2, abs(chip // 2 - middle)))
    return [[2 * chip + side for chip in order for side in range(2)]]


def exchange(x, order):
    return lax.all_to_all(x, "seq", split_axis=0, concat_axis=0, tiled=True, axis_index_groups=order)


def local(
    prefix_latent,
    block_order,
    key_up,
    value_up,
    queries,
    new_keys,
    new_values,
    suffix_keys,
    suffix_values,
    suffix_len,
):
    count = lax.axis_size("seq")
    prefix = prefix_latent.shape[0] * count
    core = (lax.axis_index("seq") % 2).astype(jnp.int32)[None]
    swap = [(i, i ^ 1) for i in range(count)]
    send, own, new_rot = rotate_queries(queries, new_keys, suffix_len, prefix, count)
    other_latent = lax.ppermute(prefix_latent, "seq", swap)
    other_order = lax.ppermute(block_order, "seq", swap)
    order = exchange_order(count)
    gathered = exchange(send, order)
    projected = project(core, block_order, other_order, prefix_latent, other_latent, key_up, value_up)
    parts = attend(gathered, *projected)
    got = exchange(parts, order)
    new_pad = jnp.pad(new_values[0], ((0, 16 - STEPS), (0, 0)))
    acc, peak, total = suffix(suffix_len, own, new_rot, new_pad, suffix_keys, suffix_values)
    return combine(got, acc, peak, total)


def solution(mesh):
    placed = (
        P(("parts", "seq"), None),
        P(("parts", "seq")),
        P(),
        P(),
        P(("parts", "seq"), None, None),
        P(("parts", "seq"), None, None),
        P(("parts", "seq"), None, None),
        P(("parts", "seq"), None, None),
        P(("parts", "seq"), None, None),
        P(("parts", "seq")),
    )
    return jax.shard_map(
        local,
        mesh=mesh,
        in_specs=placed,
        out_specs=P(("parts", "seq"), None, None),
        check_vma=False,
    )
```

```python
import functools
import math

import jax
import jax.numpy as jnp
import numpy as np
from jax import lax
from jax.experimental import pallas as pl
from jax.experimental.pallas import tpu as pltpu
from jax.sharding import PartitionSpec as P

HD = 128
QH = 32
KVH = 4
BLK = 128
STEPS = 4
SUF = 4096
GROUP = QH // KVH
HALF_KV = KVH // 2
WIDE = HALF_KV * HD
KROWS = GROUP * STEPS
HROWS = HALF_KV * KROWS
ROWS = KVH * KROWS
PAY = HROWS + 8
SCALE = 1.0 / math.sqrt(HD)
EXP2 = SCALE * math.log2(math.e)
TURN = 2.0 * math.pi / 16777216.0
SUF_TILE = 1024
PER = 15
Q_GROUP = 16
CHUNKS = 5
NEAR = 1
LATE = 3
F32 = jnp.float32
BF16 = jnp.bfloat16


def multipliers():
    half = HD // 2
    index = np.arange(half)
    freq = 500000.0 ** (-2.0 * index / (2 * half))
    return np.floor(2.0**24 * freq / (2 * np.pi)).astype(np.int64)


def phase_rows():
    mult = np.tile(multipliers(), 2)
    table = np.zeros((8, HD), np.int32)
    table[0] = mult >> 12
    table[1] = mult & 4095
    return table


def row_tables():
    mult = np.tile(multipliers(), 2)
    turns = (np.arange(BLK)[:, None] * mult[None, :]) % 16777216
    angle = turns * (2.0 * np.pi / 16777216.0)
    sign = np.where(np.arange(HD) < HD // 2, -1.0, 1.0)
    return (np.cos(angle).astype(np.float32), (np.sin(angle) * sign).astype(np.float32))


def phases(spot, high, low):
    first = spot * low
    second = (spot * high) & 4095
    turns = (first + second * 4096) & 16777215
    return turns.astype(F32) * TURN


def lane_sign(shape):
    lane = lax.broadcasted_iota(jnp.int32, shape, len(shape) - 1)
    return jnp.where(lane < HD // 2, -1.0, 1.0).astype(F32)


def turn(x, cosine, sine):
    return x * cosine + pltpu.roll(x, HD // 2, axis=1) * sine


def query_kernel(prefix, count, len_ref, table_ref, q_ref, nk_ref, send_ref, own_ref, new_ref, rows_ref, nrows_ref):
    step = lax.broadcasted_iota(jnp.int32, (8, HD), 0) % STEPS
    spot = prefix + jnp.broadcast_to(len_ref[...][None], (8, HD)) + step
    angle = phases(spot, table_ref[0:1, :], table_ref[1:2, :])
    cosine = jnp.cos(angle)
    sine = jnp.sin(angle) * lane_sign((8, HD))
    q = q_ref[0].astype(F32)
    for h in range(QH):
        rows_ref[h * STEPS : (h + 1) * STEPS, :] = q[:, h * HD : (h + 1) * HD]
    for i in range(ROWS // 8):
        rows_ref[i * 8 : i * 8 + 8, :] = turn(rows_ref[i * 8 : i * 8 + 8, :], cosine, sine)
    rotated = rows_ref[...].astype(BF16)
    own_ref[...] = rotated
    for d in range(count):
        part = d % 2
        send_ref[d] = rotated[part * HROWS : (part + 1) * HROWS]
    nrows_ref[...] = jnp.zeros_like(nrows_ref)
    nk = nk_ref[0].astype(F32)
    for k in range(KVH):
        cut = slice(k * HD, (k + 1) * HD)
        nrows_ref[0:STEPS, cut] = turn(nk[:, cut], cosine[0:STEPS], sine[0:STEPS])
    new_ref[...] = nrows_ref[...].astype(BF16)


def rotate_queries(queries, new_keys, suffix_len, prefix, count):
    vmem = pl.BlockSpec(memory_space=pltpu.VMEM)
    return pl.pallas_call(
        functools.partial(query_kernel, prefix, count),
        out_shape=(
            jax.ShapeDtypeStruct((count, HROWS, HD), BF16),
            jax.ShapeDtypeStruct((ROWS, HD), BF16),
            jax.ShapeDtypeStruct((16, KVH * HD), BF16),
        ),
        in_specs=[vmem] * 4,
        out_specs=(vmem, vmem, vmem),
        scratch_shapes=[pltpu.VMEM((ROWS, HD), F32), pltpu.VMEM((16, KVH * HD), F32)],
        name="rotate_queries",
    )(suffix_len, jnp.asarray(phase_rows()), queries, new_keys)


def project_kernel(
    core_ref,
    order0_ref,
    order1_ref,
    lat0_hbm,
    lat1_hbm,
    ku_hbm,
    vu_hbm,
    table_ref,
    rc_ref,
    rs_ref,
    k0_ref,
    v0_ref,
    v0_hbm,
    k_hbm,
    v_hbm,
    bc_ref,
    bs_ref,
    lat_ref,
    w_ref,
    rest_ref,
    k_ref,
    v_ref,
    in_sem,
    w_sem,
    out_sem,
):
    pre_rows = lat0_hbm.shape[0]
    blocks = pre_rows // BLK
    per = max(d for d in range(1, PER + 1) if blocks % d == 0)
    chunks = blocks // per
    size = per * BLK
    mine = pl.ds(pl.multiple_of(core_ref[0] * WIDE, WIDE), WIDE)
    loads = [
        pltpu.make_async_copy(ku_hbm.at[:, mine], w_ref.at[:, 0:WIDE], w_sem.at[0]),
        pltpu.make_async_copy(vu_hbm.at[:, mine], w_ref.at[:, WIDE : 2 * WIDE], w_sem.at[1]),
    ]
    fetches = []
    for side, source in enumerate((lat0_hbm, lat1_hbm)):
        for c in range(chunks):
            at = pl.ds(c * size, size)
            slot = side * chunks + c
            fetches.append(pltpu.make_async_copy(source.at[at], lat_ref.at[pl.ds(slot * size, size)], in_sem.at[slot]))
    loads[0].start()
    fetches[0].start()
    loads[1].start()
    for fetch in fetches[1:]:
        fetch.start()
    pad = bc_ref.shape[0]
    narrow = lax.broadcasted_iota(jnp.int32, (pad, blocks), 1)
    tall = lax.broadcasted_iota(jnp.int32, (pad, blocks), 0)
    spot = jnp.zeros((pad, 1), F32)
    for side, order_ref in enumerate((order0_ref, order1_ref)):
        order = jnp.broadcast_to(order_ref[...].astype(F32), (pad, blocks))
        spot = spot + jnp.sum(jnp.where(tall == side * blocks + narrow, order, 0.0), -1, keepdims=True)
    spot = jnp.broadcast_to(spot.astype(jnp.int32), (pad, HD))
    angle = phases(spot * BLK, table_ref[0:1, :], table_ref[1:2, :])
    bc_ref[...] = jnp.cos(angle)
    bs_ref[...] = jnp.sin(angle) * lane_sign((pad, HD))
    loads[0].wait()
    loads[1].wait()
    stores = []
    for slot in range(2 * chunks):
        at = pl.ds(slot * size, size)
        fetches[slot].wait()
        lat = lat_ref[at, :]
        keys = jnp.dot(lat, w_ref[...], preferred_element_type=F32)
        values = keys[:, WIDE:].astype(BF16)
        v_ref[at, :] = values[:, HD:]
        low, high = slot * size, (slot + 1) * size
        split = min(max(v0_ref.shape[0], low), high)
        if low < split:
            v0_ref[low:split, :] = values[: split - low, :HD]
        moves = [(k_ref.at[at], k_hbm.at[at]), (v_ref.at[at], v_hbm.at[at])]
        if split < high:
            rest = pl.ds(split - v0_ref.shape[0], high - split)
            rest_ref[rest, :] = values[split - low :, :HD]
            moves.append((rest_ref.at[rest], v0_hbm.at[rest]))
        for i in range(per):
            b = slot * per + i
            block_cos = bc_ref[b : b + 1, :]
            block_sin = bs_ref[b : b + 1, :]
            cosine = block_cos * rc_ref[...] - block_sin * rs_ref[...]
            sine = block_sin * rc_ref[...] + block_cos * rs_ref[...]
            for target, k in ((k0_ref, 0), (k_ref, 1)):
                part = keys[i * BLK : (i + 1) * BLK, k * HD : (k + 1) * HD]
                target[b * BLK : (b + 1) * BLK, :] = turn(part, cosine, sine).astype(BF16)
        for kind, (source, target) in enumerate(moves):
            store = pltpu.make_async_copy(source, target, out_sem.at[slot * 3 + kind])
            store.start()
            stores.append(store)
    for store in stores:
        store.wait()


def project(core, order0, order1, latent0, latent1, key_up, value_up):
    pre_rows, rank = latent0.shape
    blocks = pre_rows // BLK
    per = max(d for d in range(1, PER + 1) if blocks % d == 0)
    slots = 2 * blocks // per
    rows = 2 * pre_rows
    rc, rs = row_tables()
    smem = pl.BlockSpec(memory_space=pltpu.SMEM)
    vmem = pl.BlockSpec(memory_space=pltpu.VMEM)
    hbm = pl.BlockSpec(memory_space=pl.ANY)
    pad = -(-2 * blocks // 8) * 8
    out = jax.ShapeDtypeStruct((rows, HD), BF16)
    out_far = pltpu.HBM((rows, HD), BF16)
    close = rows // CHUNKS * NEAR
    return pl.pallas_call(
        project_kernel,
        out_shape=(out, jax.ShapeDtypeStruct((close, HD), BF16), pltpu.HBM((rows - close, HD), BF16), out_far, out_far),
        in_specs=[smem, vmem, vmem, hbm, hbm, hbm, hbm, vmem, vmem, vmem],
        out_specs=(vmem, vmem, hbm, hbm, hbm),
        scratch_shapes=[
            pltpu.VMEM((pad, HD), F32),
            pltpu.VMEM((pad, HD), F32),
            pltpu.VMEM((rows, rank), BF16),
            pltpu.VMEM((rank, 2 * WIDE), BF16),
            pltpu.VMEM((rows - close, HD), BF16),
            pltpu.VMEM((rows, HD), BF16),
            pltpu.VMEM((rows, HD), BF16),
            pltpu.SemaphoreType.DMA((slots,)),
            pltpu.SemaphoreType.DMA((2,)),
            pltpu.SemaphoreType.DMA((slots * 3,)),
        ],
        cost_estimate=pl.CostEstimate(
            flops=4 * rows * rank * WIDE, bytes_accessed=rows * (rank + 2 * WIDE) * 2, transcendentals=0
        ),
        compiler_params=pltpu.CompilerParams(vmem_limit_bytes=40 << 20),
        name="project",
    )(
        core,
        far(order0[None]),
        order1[None],
        far(latent0),
        latent1,
        far(key_up),
        far(value_up),
        far(jnp.asarray(phase_rows())),
        far(jnp.asarray(rc)),
        far(jnp.asarray(rs)),
    )


def far(x):
    return pltpu.with_memory_space_constraint(x, pltpu.HBM)


def three(x):
    first = x.astype(BF16).astype(F32)
    rest = x - first
    second = rest.astype(BF16).astype(F32)
    return first, second, rest - second


def attend_kernel(per, q_ref, k0_ref, v0_ref, v0_hbm, k_hbm, v_hbm, out_ref, rest_ref, k_ref, v_ref, stat_ref, sem):
    nt = (((1,), (1,)), ((), ()))
    row = lax.broadcasted_iota(jnp.int32, (KROWS, HD), 0)
    lane = lax.broadcasted_iota(jnp.int32, (KROWS, HD), 1)
    place = lax.broadcasted_iota(jnp.int32, (8, HD), 0)
    fetches = [
        pltpu.make_async_copy(v0_hbm, rest_ref, sem.at[0]),
        pltpu.make_async_copy(k_hbm, k_ref, sem.at[1]),
        pltpu.make_async_copy(v_hbm, v_ref, sem.at[2]),
    ]
    for fetch in fetches:
        fetch.start()

    for k in range(HALF_KV):
        if k and LATE < 0:
            fetches[1].wait()
            fetches[2].wait()
        keys = (k0_ref, k_ref)[k]

        def group(g, first=False, k=k, keys=keys):
            base = g * per
            rows = slice(k * KROWS, (k + 1) * KROWS)
            q = q_ref[pl.ds(base, per), rows, :].reshape(per * KROWS, HD)
            width = k_hbm.shape[0] // CHUNKS

            def score(c):
                return lax.dot_general(q, keys[c * width : (c + 1) * width, :], nt, preferred_element_type=F32)

            ahead = score(0)
            for c in range(CHUNKS):
                s = ahead
                if c + 1 < CHUNKS:
                    ahead = score(c + 1)
                best = jnp.max(s, -1, keepdims=True)
                if first and c == NEAR:
                    fetches[0].wait()
                if first and c == LATE:
                    fetches[1].wait()
                    fetches[2].wait()
                if c:
                    best = jnp.maximum(peak, best)
                    keep = jnp.exp2((peak - best) * EXP2)
                e = jnp.exp2((s - best) * EXP2)
                here = jnp.sum(e, -1, keepdims=True)
                if k:
                    values = v_ref[c * width : (c + 1) * width, :]
                elif c < NEAR:
                    values = v0_ref[c * width : (c + 1) * width, :]
                else:
                    values = rest_ref[(c - NEAR) * width : (c - NEAR + 1) * width, :]
                o = jnp.dot(e.astype(BF16), values, preferred_element_type=F32)
                total = total * keep + here if c else here
                acc = acc * keep + o if c else o
                peak = best
            o = acc / total
            out_ref[pl.ds(base, per), rows, :] = o.astype(BF16).reshape(per, KROWS, HD)
            peak = peak * EXP2
            for r in range(per):
                cut = slice(r * KROWS, (r + 1) * KROWS)
                stats = jnp.zeros((8, HD), F32)
                for i, part in enumerate((peak, total)):
                    spread = jnp.where(lane == row + k * KROWS, part[cut], 0.0)
                    for j, line in enumerate(three(jnp.sum(spread, 0, keepdims=True))):
                        stats = jnp.where(place == 3 * i + j, line, stats)
                if k == 0:
                    stat_ref[base + r] = stats
                else:
                    out_ref[base + r, HROWS:PAY, :] = (stat_ref[base + r] + stats).astype(BF16)

        group(0, k == 0)
        groups = q_ref.shape[0] // per
        if groups > 1:
            pl.loop(1, groups)(group)


def attend(q, k0, v0, rest, k1, v1):
    count = q.shape[0]
    rows = k0.shape[0]
    vmem = pl.BlockSpec(memory_space=pltpu.VMEM)
    hbm = pl.BlockSpec(memory_space=pl.ANY)
    return pl.pallas_call(
        functools.partial(attend_kernel, math.gcd(count, Q_GROUP)),
        out_shape=jax.ShapeDtypeStruct((count, PAY, HD), BF16),
        in_specs=[vmem, vmem, vmem, hbm, hbm, hbm],
        out_specs=vmem,
        scratch_shapes=[
            pltpu.VMEM(rest.shape, BF16),
            pltpu.VMEM((rows, HD), BF16),
            pltpu.VMEM((rows, HD), BF16),
            pltpu.VMEM((count, 8, HD), F32),
            pltpu.SemaphoreType.DMA((3,)),
        ],
        compiler_params=pltpu.CompilerParams(vmem_limit_bytes=48 << 20),
        cost_estimate=pl.CostEstimate(
            flops=4 * count * HROWS * HD * rows,
            bytes_accessed=4 * rows * WIDE,
            transcendentals=count * HROWS * rows,
        ),
        name="attend",
    )(q, k0, v0, far(rest), far(k1), far(v1))


def suffix_kernel(len_ref, q_ref, nk_ref, nv_ref, k_ref, v_ref, acc_ref, peak_ref, total_ref):
    step = pl.program_id(0)
    length = len_ref[0]
    tile = k_ref.shape[1]
    nt = (((1,), (1,)), ((), ()))

    def scores(keys):
        return jnp.concatenate(
            [
                lax.dot_general(
                    q_ref[k * KROWS : (k + 1) * KROWS, :],
                    keys[:, k * HD : (k + 1) * HD],
                    nt,
                    preferred_element_type=F32,
                )
                for k in range(KVH)
            ],
            0,
        )

    def weigh(probs, values):
        probs = probs.astype(BF16)
        return jnp.concatenate(
            [
                jnp.dot(
                    probs[k * KROWS : (k + 1) * KROWS],
                    values[:, k * HD : (k + 1) * HD],
                    preferred_element_type=F32,
                )
                for k in range(KVH)
            ],
            0,
        )

    @pl.when(step == 0)
    def _():
        s = scores(nk_ref[...])
        row = lax.broadcasted_iota(jnp.int32, s.shape, 0) % STEPS
        lane = lax.broadcasted_iota(jnp.int32, s.shape, 1)
        s = jnp.where(lane <= row, s, -jnp.inf)
        peak = jnp.max(s, -1, keepdims=True)
        e = jnp.exp2((s - peak) * EXP2)
        acc_ref[...] = weigh(e, nv_ref[...])
        peak_ref[...] = jnp.broadcast_to(peak, peak_ref.shape)
        total_ref[...] = jnp.broadcast_to(jnp.sum(e, -1, keepdims=True), total_ref.shape)

    @pl.when(step * tile < length)
    def _():
        s = scores(k_ref[0])
        spot = step * tile + lax.broadcasted_iota(jnp.int32, s.shape, 1)
        s = jnp.where(spot < length, s, -jnp.inf)
        old = peak_ref[:, 0:1]
        peak = jnp.maximum(old, jnp.max(s, -1, keepdims=True))
        keep = jnp.exp2((old - peak) * EXP2)
        e = jnp.exp2((s - peak) * EXP2)
        acc_ref[...] = acc_ref[...] * keep + weigh(e, v_ref[0])
        total_ref[...] = total_ref[...] * keep + jnp.sum(e, -1, keepdims=True)
        peak_ref[...] = jnp.broadcast_to(peak, peak_ref.shape)

    @pl.when(step == pl.num_programs(0) - 1)
    def _():
        peak_ref[...] = peak_ref[...] * EXP2


def suffix(length, q, new_rot, new_values, keys, values):
    tile = SUF_TILE
    fixed = lambda i, n: (0, 0)
    walk = lambda i, n: (0, jnp.minimum(i, (n[0] - 1) // tile), 0)
    out = jax.ShapeDtypeStruct((ROWS, HD), F32)
    return pl.pallas_call(
        suffix_kernel,
        out_shape=(out, out, out),
        grid_spec=pltpu.PrefetchScalarGridSpec(
            num_scalar_prefetch=1,
            grid=(SUF // tile,),
            in_specs=[
                pl.BlockSpec((ROWS, HD), fixed),
                pl.BlockSpec((16, KVH * HD), fixed),
                pl.BlockSpec((16, KVH * HD), fixed),
                pl.BlockSpec((1, tile, KVH * HD), walk),
                pl.BlockSpec((1, tile, KVH * HD), walk),
            ],
            out_specs=[pl.BlockSpec((ROWS, HD), fixed)] * 3,
        ),
        cost_estimate=pl.CostEstimate(
            flops=4 * ROWS * SUF * HD, bytes_accessed=4 * SUF * KVH * HD, transcendentals=ROWS * SUF
        ),
        compiler_params=pltpu.CompilerParams(vmem_limit_bytes=40 << 20),
        name="suffix",
    )(length, q, new_rot, new_values, far(keys), far(values))


def combine_kernel(got_ref, acc_ref, peak_ref, total_ref, out_ref):
    count = got_ref.shape[0]
    row = lax.broadcasted_iota(jnp.int32, (HROWS, HD), 0)
    lane = lax.broadcasted_iota(jnp.int32, (HROWS, HD), 1)
    eye = row == lane

    def column(line):
        return jnp.sum(jnp.where(eye, line, 0.0), -1, keepdims=True)

    for part in range(2):
        sources = range(part, count, 2)
        stats = [got_ref[j, HROWS:PAY, :].astype(F32) for j in sources]
        peaks = [s[0:1] + s[1:2] + s[2:3] for s in stats]
        totals = [s[3:4] + s[4:5] + s[5:6] for s in stats]
        top = functools.reduce(jnp.maximum, peaks)
        factors = [t * jnp.exp2(p - top) for p, t in zip(peaks, totals)]
        denom = column(sum(factors))
        top = column(top)
        numer = jnp.zeros((HROWS, HD), F32)
        for j, factor in zip(sources, factors):
            numer = numer + column(factor) * got_ref[j, 0:HROWS, :].astype(F32)
        cut = slice(part * HROWS, (part + 1) * HROWS)
        near = peak_ref[cut, :]
        big = jnp.maximum(top, near)
        far_weight = jnp.exp2(top - big)
        near_weight = jnp.exp2(near - big)
        result = (numer * far_weight + acc_ref[cut, :] * near_weight) / (
            denom * far_weight + total_ref[cut, :] * near_weight
        )
        for h in range(HROWS // STEPS):
            at = part * (HROWS // STEPS) + h
            out_ref[0, :, at * HD : (at + 1) * HD] = result[h * STEPS : (h + 1) * STEPS].astype(BF16)


def combine(got, acc, peak, total):
    vmem = pl.BlockSpec(memory_space=pltpu.VMEM)
    return pl.pallas_call(
        combine_kernel,
        out_shape=jax.ShapeDtypeStruct((1, STEPS, QH * HD), BF16),
        in_specs=[vmem] * 4,
        out_specs=vmem,
        compiler_params=pltpu.CompilerParams(vmem_limit_bytes=8 << 20),
        name="combine",
    )(got, acc, peak, total)


def exchange_order(count):
    chips = count // 2
    middle = chips // 2 / 2 - 0.4
    order = sorted(range(chips), key=lambda chip: (1 - chip % 2, abs(chip // 2 - middle)))
    return [[2 * chip + side for chip in order for side in range(2)]]


def exchange(x, order):
    return lax.all_to_all(x, "seq", split_axis=0, concat_axis=0, tiled=True, axis_index_groups=order)


def local(
    prefix_latent,
    block_order,
    key_up,
    value_up,
    queries,
    new_keys,
    new_values,
    suffix_keys,
    suffix_values,
    suffix_len,
):
    count = lax.axis_size("seq")
    prefix = prefix_latent.shape[0] * count
    core = (lax.axis_index("seq") % 2).astype(jnp.int32)[None]
    swap = [(i, i ^ 1) for i in range(count)]
    send, own, new_rot = rotate_queries(queries, new_keys, suffix_len, prefix, count)
    other_latent = lax.ppermute(prefix_latent, "seq", swap)
    other_order = lax.ppermute(block_order, "seq", swap)
    order = exchange_order(count)
    gathered = exchange(send, order)
    projected = project(core, block_order, other_order, prefix_latent, other_latent, key_up, value_up)
    parts = attend(gathered, *projected)
    got = exchange(parts, order)
    new_pad = jnp.pad(new_values[0], ((0, 16 - STEPS), (0, 0)))
    acc, peak, total = suffix(suffix_len, own, new_rot, new_pad, suffix_keys, suffix_values)
    return combine(got, acc, peak, total)


def solution(mesh):
    placed = (
        P(("parts", "seq"), None),
        P(("parts", "seq")),
        P(),
        P(),
        P(("parts", "seq"), None, None),
        P(("parts", "seq"), None, None),
        P(("parts", "seq"), None, None),
        P(("parts", "seq"), None, None),
        P(("parts", "seq"), None, None),
        P(("parts", "seq")),
    )
    return jax.shard_map(
        local,
        mesh=mesh,
        in_specs=placed,
        out_specs=P(("parts", "seq"), None, None),
        check_vma=False,
    )
```

```python
import functools
import math

import jax
import jax.numpy as jnp
import numpy as np
from jax import lax
from jax.experimental import pallas as pl
from jax.experimental.pallas import tpu as pltpu
from jax.sharding import PartitionSpec as P

HD = 128
QH = 32
KVH = 4
BLK = 128
STEPS = 4
SUF = 4096
GROUP = QH // KVH
HALF_KV = KVH // 2
WIDE = HALF_KV * HD
KROWS = GROUP * STEPS
HROWS = HALF_KV * KROWS
ROWS = KVH * KROWS
PAY = HROWS + 8
SCALE = 1.0 / math.sqrt(HD)
EXP2 = SCALE * math.log2(math.e)
TURN = 2.0 * math.pi / 16777216.0
SUF_TILE = 1024
PER = 15
Q_GROUP = 16
CHUNKS = 5
NEAR = 1
LATE = 2
F32 = jnp.float32
BF16 = jnp.bfloat16


def multipliers():
    half = HD // 2
    index = np.arange(half)
    freq = 500000.0 ** (-2.0 * index / (2 * half))
    return np.floor(2.0**24 * freq / (2 * np.pi)).astype(np.int64)


def phase_rows():
    mult = np.tile(multipliers(), 2)
    table = np.zeros((8, HD), np.int32)
    table[0] = mult >> 12
    table[1] = mult & 4095
    return table


def row_tables():
    mult = np.tile(multipliers(), 2)
    turns = (np.arange(BLK)[:, None] * mult[None, :]) % 16777216
    angle = turns * (2.0 * np.pi / 16777216.0)
    sign = np.where(np.arange(HD) < HD // 2, -1.0, 1.0)
    return (np.cos(angle).astype(np.float32), (np.sin(angle) * sign).astype(np.float32))


def phases(spot, high, low):
    first = spot * low
    second = (spot * high) & 4095
    turns = (first + second * 4096) & 16777215
    return turns.astype(F32) * TURN


def lane_sign(shape):
    lane = lax.broadcasted_iota(jnp.int32, shape, len(shape) - 1)
    return jnp.where(lane < HD // 2, -1.0, 1.0).astype(F32)


def turn(x, cosine, sine):
    return x * cosine + pltpu.roll(x, HD // 2, axis=1) * sine


def query_kernel(prefix, count, len_ref, table_ref, q_ref, nk_ref, send_ref, own_ref, new_ref, rows_ref, nrows_ref):
    step = lax.broadcasted_iota(jnp.int32, (8, HD), 0) % STEPS
    spot = prefix + jnp.broadcast_to(len_ref[...][None], (8, HD)) + step
    angle = phases(spot, table_ref[0:1, :], table_ref[1:2, :])
    cosine = jnp.cos(angle)
    sine = jnp.sin(angle) * lane_sign((8, HD))
    q = q_ref[0].astype(F32)
    for h in range(QH):
        rows_ref[h * STEPS : (h + 1) * STEPS, :] = q[:, h * HD : (h + 1) * HD]
    for i in range(ROWS // 8):
        rows_ref[i * 8 : i * 8 + 8, :] = turn(rows_ref[i * 8 : i * 8 + 8, :], cosine, sine)
    rotated = rows_ref[...].astype(BF16)
    own_ref[...] = rotated
    for d in range(count):
        part = d % 2
        send_ref[d] = rotated[part * HROWS : (part + 1) * HROWS]
    nrows_ref[...] = jnp.zeros_like(nrows_ref)
    nk = nk_ref[0].astype(F32)
    for k in range(KVH):
        cut = slice(k * HD, (k + 1) * HD)
        nrows_ref[0:STEPS, cut] = turn(nk[:, cut], cosine[0:STEPS], sine[0:STEPS])
    new_ref[...] = nrows_ref[...].astype(BF16)


def rotate_queries(queries, new_keys, suffix_len, prefix, count):
    vmem = pl.BlockSpec(memory_space=pltpu.VMEM)
    return pl.pallas_call(
        functools.partial(query_kernel, prefix, count),
        out_shape=(
            jax.ShapeDtypeStruct((count, HROWS, HD), BF16),
            jax.ShapeDtypeStruct((ROWS, HD), BF16),
            jax.ShapeDtypeStruct((16, KVH * HD), BF16),
        ),
        in_specs=[vmem] * 4,
        out_specs=(vmem, vmem, vmem),
        scratch_shapes=[pltpu.VMEM((ROWS, HD), F32), pltpu.VMEM((16, KVH * HD), F32)],
        name="rotate_queries",
    )(suffix_len, jnp.asarray(phase_rows()), queries, new_keys)


def project_kernel(
    core_ref,
    order0_ref,
    order1_ref,
    lat0_hbm,
    lat1_hbm,
    ku_hbm,
    vu_hbm,
    table_ref,
    rc_ref,
    rs_ref,
    k0_ref,
    v0_ref,
    v0_hbm,
    k_hbm,
    v_hbm,
    bc_ref,
    bs_ref,
    lat_ref,
    w_ref,
    rest_ref,
    k_ref,
    v_ref,
    in_sem,
    w_sem,
    out_sem,
):
    pre_rows = lat0_hbm.shape[0]
    blocks = pre_rows // BLK
    per = max(d for d in range(1, PER + 1) if blocks % d == 0)
    chunks = blocks // per
    size = per * BLK
    mine = pl.ds(pl.multiple_of(core_ref[0] * WIDE, WIDE), WIDE)
    loads = [
        pltpu.make_async_copy(ku_hbm.at[:, mine], w_ref.at[:, 0:WIDE], w_sem.at[0]),
        pltpu.make_async_copy(vu_hbm.at[:, mine], w_ref.at[:, WIDE : 2 * WIDE], w_sem.at[1]),
    ]
    fetches = []
    for side, source in enumerate((lat0_hbm, lat1_hbm)):
        for c in range(chunks):
            at = pl.ds(c * size, size)
            slot = side * chunks + c
            fetches.append(pltpu.make_async_copy(source.at[at], lat_ref.at[pl.ds(slot * size, size)], in_sem.at[slot]))
    loads[0].start()
    fetches[0].start()
    loads[1].start()
    for fetch in fetches[1:]:
        fetch.start()
    pad = bc_ref.shape[0]
    narrow = lax.broadcasted_iota(jnp.int32, (pad, blocks), 1)
    tall = lax.broadcasted_iota(jnp.int32, (pad, blocks), 0)
    spot = jnp.zeros((pad, 1), F32)
    for side, order_ref in enumerate((order0_ref, order1_ref)):
        order = jnp.broadcast_to(order_ref[...].astype(F32), (pad, blocks))
        spot = spot + jnp.sum(jnp.where(tall == side * blocks + narrow, order, 0.0), -1, keepdims=True)
    spot = jnp.broadcast_to(spot.astype(jnp.int32), (pad, HD))
    angle = phases(spot * BLK, table_ref[0:1, :], table_ref[1:2, :])
    bc_ref[...] = jnp.cos(angle)
    bs_ref[...] = jnp.sin(angle) * lane_sign((pad, HD))
    loads[0].wait()
    loads[1].wait()
    stores = []
    for slot in range(2 * chunks):
        at = pl.ds(slot * size, size)
        fetches[slot].wait()
        lat = lat_ref[at, :]
        keys = jnp.dot(lat, w_ref[...], preferred_element_type=F32)
        values = keys[:, WIDE:].astype(BF16)
        v_ref[at, :] = values[:, HD:]
        low, high = slot * size, (slot + 1) * size
        split = min(max(v0_ref.shape[0], low), high)
        if low < split:
            v0_ref[low:split, :] = values[: split - low, :HD]
        moves = [(k_ref.at[at], k_hbm.at[at]), (v_ref.at[at], v_hbm.at[at])]
        if split < high:
            rest = pl.ds(split - v0_ref.shape[0], high - split)
            rest_ref[rest, :] = values[split - low :, :HD]
            moves.append((rest_ref.at[rest], v0_hbm.at[rest]))
        for i in range(per):
            b = slot * per + i
            block_cos = bc_ref[b : b + 1, :]
            block_sin = bs_ref[b : b + 1, :]
            cosine = block_cos * rc_ref[...] - block_sin * rs_ref[...]
            sine = block_sin * rc_ref[...] + block_cos * rs_ref[...]
            for target, k in ((k0_ref, 0), (k_ref, 1)):
                part = keys[i * BLK : (i + 1) * BLK, k * HD : (k + 1) * HD]
                target[b * BLK : (b + 1) * BLK, :] = turn(part, cosine, sine).astype(BF16)
        for kind, (source, target) in enumerate(moves):
            store = pltpu.make_async_copy(source, target, out_sem.at[slot * 3 + kind])
            store.start()
            stores.append(store)
    for store in stores:
        store.wait()


def project(core, order0, order1, latent0, latent1, key_up, value_up):
    pre_rows, rank = latent0.shape
    blocks = pre_rows // BLK
    per = max(d for d in range(1, PER + 1) if blocks % d == 0)
    slots = 2 * blocks // per
    rows = 2 * pre_rows
    rc, rs = row_tables()
    smem = pl.BlockSpec(memory_space=pltpu.SMEM)
    vmem = pl.BlockSpec(memory_space=pltpu.VMEM)
    hbm = pl.BlockSpec(memory_space=pl.ANY)
    pad = -(-2 * blocks // 8) * 8
    out = jax.ShapeDtypeStruct((rows, HD), BF16)
    out_far = pltpu.HBM((rows, HD), BF16)
    close = rows // CHUNKS * NEAR
    return pl.pallas_call(
        project_kernel,
        out_shape=(out, jax.ShapeDtypeStruct((close, HD), BF16), pltpu.HBM((rows - close, HD), BF16), out_far, out_far),
        in_specs=[smem, vmem, vmem, hbm, hbm, hbm, hbm, vmem, vmem, vmem],
        out_specs=(vmem, vmem, hbm, hbm, hbm),
        scratch_shapes=[
            pltpu.VMEM((pad, HD), F32),
            pltpu.VMEM((pad, HD), F32),
            pltpu.VMEM((rows, rank), BF16),
            pltpu.VMEM((rank, 2 * WIDE), BF16),
            pltpu.VMEM((rows - close, HD), BF16),
            pltpu.VMEM((rows, HD), BF16),
            pltpu.VMEM((rows, HD), BF16),
            pltpu.SemaphoreType.DMA((slots,)),
            pltpu.SemaphoreType.DMA((2,)),
            pltpu.SemaphoreType.DMA((slots * 3,)),
        ],
        cost_estimate=pl.CostEstimate(
            flops=4 * rows * rank * WIDE, bytes_accessed=rows * (rank + 2 * WIDE) * 2, transcendentals=0
        ),
        compiler_params=pltpu.CompilerParams(vmem_limit_bytes=40 << 20),
        name="project",
    )(
        core,
        far(order0[None]),
        order1[None],
        far(latent0),
        latent1,
        far(key_up),
        far(value_up),
        far(jnp.asarray(phase_rows())),
        far(jnp.asarray(rc)),
        far(jnp.asarray(rs)),
    )


def far(x):
    return pltpu.with_memory_space_constraint(x, pltpu.HBM)


def three(x):
    first = x.astype(BF16).astype(F32)
    rest = x - first
    second = rest.astype(BF16).astype(F32)
    return first, second, rest - second


def attend_kernel(per, q_ref, k0_ref, v0_ref, v0_hbm, k_hbm, v_hbm, out_ref, rest_ref, k_ref, v_ref, stat_ref, sem):
    nt = (((1,), (1,)), ((), ()))
    row = lax.broadcasted_iota(jnp.int32, (KROWS, HD), 0)
    lane = lax.broadcasted_iota(jnp.int32, (KROWS, HD), 1)
    place = lax.broadcasted_iota(jnp.int32, (8, HD), 0)
    fetches = [
        pltpu.make_async_copy(v0_hbm, rest_ref, sem.at[0]),
        pltpu.make_async_copy(k_hbm, k_ref, sem.at[1]),
        pltpu.make_async_copy(v_hbm, v_ref, sem.at[2]),
    ]
    for fetch in fetches:
        fetch.start()

    for k in range(HALF_KV):
        if k and LATE < 0:
            fetches[1].wait()
            fetches[2].wait()
        keys = (k0_ref, k_ref)[k]

        def group(g, first=False, k=k, keys=keys):
            base = g * per
            rows = slice(k * KROWS, (k + 1) * KROWS)
            q = q_ref[pl.ds(base, per), rows, :].reshape(per * KROWS, HD)
            width = k_hbm.shape[0] // CHUNKS

            def score(c):
                return lax.dot_general(q, keys[c * width : (c + 1) * width, :], nt, preferred_element_type=F32)

            ahead = score(0)
            for c in range(CHUNKS):
                s = ahead
                if c + 1 < CHUNKS:
                    ahead = score(c + 1)
                best = jnp.max(s, -1, keepdims=True)
                if first and c == NEAR:
                    fetches[0].wait()
                if first and c == LATE:
                    fetches[1].wait()
                    fetches[2].wait()
                if c:
                    best = jnp.maximum(peak, best)
                    keep = jnp.exp2((peak - best) * EXP2)
                e = jnp.exp2((s - best) * EXP2)
                here = jnp.sum(e, -1, keepdims=True)
                if k:
                    values = v_ref[c * width : (c + 1) * width, :]
                elif c < NEAR:
                    values = v0_ref[c * width : (c + 1) * width, :]
                else:
                    values = rest_ref[(c - NEAR) * width : (c - NEAR + 1) * width, :]
                o = jnp.dot(e.astype(BF16), values, preferred_element_type=F32)
                total = total * keep + here if c else here
                acc = acc * keep + o if c else o
                peak = best
            o = acc / total
            out_ref[pl.ds(base, per), rows, :] = o.astype(BF16).reshape(per, KROWS, HD)
            peak = peak * EXP2
            for r in range(per):
                cut = slice(r * KROWS, (r + 1) * KROWS)
                stats = jnp.zeros((8, HD), F32)
                for i, part in enumerate((peak, total)):
                    spread = jnp.where(lane == row + k * KROWS, part[cut], 0.0)
                    for j, line in enumerate(three(jnp.sum(spread, 0, keepdims=True))):
                        stats = jnp.where(place == 3 * i + j, line, stats)
                if k == 0:
                    stat_ref[base + r] = stats
                else:
                    out_ref[base + r, HROWS:PAY, :] = (stat_ref[base + r] + stats).astype(BF16)

        group(0, k == 0)
        groups = q_ref.shape[0] // per
        if groups > 1:
            pl.loop(1, groups)(group)


def attend(q, k0, v0, rest, k1, v1):
    count = q.shape[0]
    rows = k0.shape[0]
    vmem = pl.BlockSpec(memory_space=pltpu.VMEM)
    hbm = pl.BlockSpec(memory_space=pl.ANY)
    return pl.pallas_call(
        functools.partial(attend_kernel, math.gcd(count, Q_GROUP)),
        out_shape=jax.ShapeDtypeStruct((count, PAY, HD), BF16),
        in_specs=[vmem, vmem, vmem, hbm, hbm, hbm],
        out_specs=vmem,
        scratch_shapes=[
            pltpu.VMEM(rest.shape, BF16),
            pltpu.VMEM((rows, HD), BF16),
            pltpu.VMEM((rows, HD), BF16),
            pltpu.VMEM((count, 8, HD), F32),
            pltpu.SemaphoreType.DMA((3,)),
        ],
        compiler_params=pltpu.CompilerParams(vmem_limit_bytes=48 << 20),
        cost_estimate=pl.CostEstimate(
            flops=4 * count * HROWS * HD * rows,
            bytes_accessed=4 * rows * WIDE,
            transcendentals=count * HROWS * rows,
        ),
        name="attend",
    )(q, k0, v0, far(rest), far(k1), far(v1))


def suffix_kernel(len_ref, q_ref, nk_ref, nv_ref, k_ref, v_ref, acc_ref, peak_ref, total_ref):
    step = pl.program_id(0)
    length = len_ref[0]
    tile = k_ref.shape[1]
    nt = (((1,), (1,)), ((), ()))

    def scores(keys):
        return jnp.concatenate(
            [
                lax.dot_general(
                    q_ref[k * KROWS : (k + 1) * KROWS, :],
                    keys[:, k * HD : (k + 1) * HD],
                    nt,
                    preferred_element_type=F32,
                )
                for k in range(KVH)
            ],
            0,
        )

    def weigh(probs, values):
        probs = probs.astype(BF16)
        return jnp.concatenate(
            [
                jnp.dot(
                    probs[k * KROWS : (k + 1) * KROWS],
                    values[:, k * HD : (k + 1) * HD],
                    preferred_element_type=F32,
                )
                for k in range(KVH)
            ],
            0,
        )

    @pl.when(step == 0)
    def _():
        s = scores(nk_ref[...])
        row = lax.broadcasted_iota(jnp.int32, s.shape, 0) % STEPS
        lane = lax.broadcasted_iota(jnp.int32, s.shape, 1)
        s = jnp.where(lane <= row, s, -jnp.inf)
        peak = jnp.max(s, -1, keepdims=True)
        e = jnp.exp2((s - peak) * EXP2)
        acc_ref[...] = weigh(e, nv_ref[...])
        peak_ref[...] = jnp.broadcast_to(peak, peak_ref.shape)
        total_ref[...] = jnp.broadcast_to(jnp.sum(e, -1, keepdims=True), total_ref.shape)

    @pl.when(step * tile < length)
    def _():
        s = scores(k_ref[0])
        spot = step * tile + lax.broadcasted_iota(jnp.int32, s.shape, 1)
        s = jnp.where(spot < length, s, -jnp.inf)
        old = peak_ref[:, 0:1]
        peak = jnp.maximum(old, jnp.max(s, -1, keepdims=True))
        keep = jnp.exp2((old - peak) * EXP2)
        e = jnp.exp2((s - peak) * EXP2)
        acc_ref[...] = acc_ref[...] * keep + weigh(e, v_ref[0])
        total_ref[...] = total_ref[...] * keep + jnp.sum(e, -1, keepdims=True)
        peak_ref[...] = jnp.broadcast_to(peak, peak_ref.shape)

    @pl.when(step == pl.num_programs(0) - 1)
    def _():
        peak_ref[...] = peak_ref[...] * EXP2


def suffix(length, q, new_rot, new_values, keys, values):
    tile = SUF_TILE
    fixed = lambda i, n: (0, 0)
    walk = lambda i, n: (0, jnp.minimum(i, (n[0] - 1) // tile), 0)
    out = jax.ShapeDtypeStruct((ROWS, HD), F32)
    return pl.pallas_call(
        suffix_kernel,
        out_shape=(out, out, out),
        grid_spec=pltpu.PrefetchScalarGridSpec(
            num_scalar_prefetch=1,
            grid=(SUF // tile,),
            in_specs=[
                pl.BlockSpec((ROWS, HD), fixed),
                pl.BlockSpec((16, KVH * HD), fixed),
                pl.BlockSpec((16, KVH * HD), fixed),
                pl.BlockSpec((1, tile, KVH * HD), walk),
                pl.BlockSpec((1, tile, KVH * HD), walk),
            ],
            out_specs=[pl.BlockSpec((ROWS, HD), fixed)] * 3,
        ),
        cost_estimate=pl.CostEstimate(
            flops=4 * ROWS * SUF * HD, bytes_accessed=4 * SUF * KVH * HD, transcendentals=ROWS * SUF
        ),
        compiler_params=pltpu.CompilerParams(vmem_limit_bytes=40 << 20),
        name="suffix",
    )(length, q, new_rot, new_values, far(keys), far(values))


def combine_kernel(got_ref, acc_ref, peak_ref, total_ref, out_ref):
    count = got_ref.shape[0]
    row = lax.broadcasted_iota(jnp.int32, (HROWS, HD), 0)
    lane = lax.broadcasted_iota(jnp.int32, (HROWS, HD), 1)
    eye = row == lane

    def column(line):
        return jnp.sum(jnp.where(eye, line, 0.0), -1, keepdims=True)

    for part in range(2):
        sources = range(part, count, 2)
        stats = [got_ref[j, HROWS:PAY, :].astype(F32) for j in sources]
        peaks = [s[0:1] + s[1:2] + s[2:3] for s in stats]
        totals = [s[3:4] + s[4:5] + s[5:6] for s in stats]
        top = functools.reduce(jnp.maximum, peaks)
        factors = [t * jnp.exp2(p - top) for p, t in zip(peaks, totals)]
        denom = column(sum(factors))
        top = column(top)
        numer = jnp.zeros((HROWS, HD), F32)
        for j, factor in zip(sources, factors):
            numer = numer + column(factor) * got_ref[j, 0:HROWS, :].astype(F32)
        cut = slice(part * HROWS, (part + 1) * HROWS)
        near = peak_ref[cut, :]
        big = jnp.maximum(top, near)
        far_weight = jnp.exp2(top - big)
        near_weight = jnp.exp2(near - big)
        result = (numer * far_weight + acc_ref[cut, :] * near_weight) / (
            denom * far_weight + total_ref[cut, :] * near_weight
        )
        for h in range(HROWS // STEPS):
            at = part * (HROWS // STEPS) + h
            out_ref[0, :, at * HD : (at + 1) * HD] = result[h * STEPS : (h + 1) * STEPS].astype(BF16)


def combine(got, acc, peak, total):
    vmem = pl.BlockSpec(memory_space=pltpu.VMEM)
    return pl.pallas_call(
        combine_kernel,
        out_shape=jax.ShapeDtypeStruct((1, STEPS, QH * HD), BF16),
        in_specs=[vmem] * 4,
        out_specs=vmem,
        compiler_params=pltpu.CompilerParams(vmem_limit_bytes=8 << 20),
        name="combine",
    )(got, acc, peak, total)


def exchange_order(count):
    chips = count // 2
    middle = chips // 2 / 2

    def rank(chip):
        side = chip % 2
        return 1 - side, abs(chip // 2 - (middle + (-0.4 if side else 0.4)))

    order = sorted(range(chips), key=rank)
    return [[2 * chip + side for chip in order for side in range(2)]]


def exchange(x, order):
    return lax.all_to_all(x, "seq", split_axis=0, concat_axis=0, tiled=True, axis_index_groups=order)


def local(
    prefix_latent,
    block_order,
    key_up,
    value_up,
    queries,
    new_keys,
    new_values,
    suffix_keys,
    suffix_values,
    suffix_len,
):
    count = lax.axis_size("seq")
    prefix = prefix_latent.shape[0] * count
    core = (lax.axis_index("seq") % 2).astype(jnp.int32)[None]
    swap = [(i, i ^ 1) for i in range(count)]
    send, own, new_rot = rotate_queries(queries, new_keys, suffix_len, prefix, count)
    other_latent = lax.ppermute(prefix_latent, "seq", swap)
    other_order = lax.ppermute(block_order, "seq", swap)
    order = exchange_order(count)
    gathered = exchange(send, order)
    projected = project(core, block_order, other_order, prefix_latent, other_latent, key_up, value_up)
    parts = attend(gathered, *projected)
    got = exchange(parts, order)
    new_pad = jnp.pad(new_values[0], ((0, 16 - STEPS), (0, 0)))
    acc, peak, total = suffix(suffix_len, own, new_rot, new_pad, suffix_keys, suffix_values)
    return combine(got, acc, peak, total)


def solution(mesh):
    placed = (
        P(("parts", "seq"), None),
        P(("parts", "seq")),
        P(),
        P(),
        P(("parts", "seq"), None, None),
        P(("parts", "seq"), None, None),
        P(("parts", "seq"), None, None),
        P(("parts", "seq"), None, None),
        P(("parts", "seq"), None, None),
        P(("parts", "seq")),
    )
    return jax.shard_map(
        local,
        mesh=mesh,
        in_specs=placed,
        out_specs=P(("parts", "seq"), None, None),
        check_vma=False,
    )
```
